32 devices in a mesh: subtree: 8 (over z, core), front: 4 (over y, x).
Axes of the slice: x: 2, y: 2, z: 4, core: 2. Of those that a mesh axis runs over, the one named last changes fastest.
Arguments:
- leaf_rhs: float32 [8, 2048, 256], P('subtree', 'front'), may hold values from -6 to 6
- mid_rhs: float32 [2, 4096, 256], P(None, 'front'), may hold values from -6 to 6
- root_rhs: float32 [10240, 256], P('front'), may hold values from -6 to 6
- leaf_lower: float32 [8, 2048, 2048], P('subtree', None, 'front'), may hold values from -0.125 to 0.125
- leaf_below: float32 [8, 2048, 2048], P('subtree', None, 'front'), may hold values from -0.125 to 0.125
- leaf_right: float32 [8, 2048, 2048], P('subtree', None, 'front'), may hold values from -0.125 to 0.125
- leaf_upper: float32 [8, 2048, 2048], P('subtree', None, 'front'), may hold values from -0.125 to 0.125
- mid_lower: float32 [2, 4096, 4096], P(None, 'subtree', 'front'), may hold values from -0.09375 to 0.09375
- mid_below: float32 [2, 4096, 4096], P(None, 'front', 'subtree'), may hold values from -0.09375 to 0.09375
- mid_right: float32 [2, 4096, 4096], P(None, 'subtree', 'front'), may hold values from -0.09375 to 0.09375
- mid_upper: float32 [2, 4096, 4096], P(None, 'front', 'subtree'), may hold values from -0.09375 to 0.09375
- root_lower: float32 [10240, 10240], P('subtree', 'front'), may hold values from -0.0625 to 0.0625
- root_upper: float32 [10240, 10240], P('front', 'subtree'), may hold values from -0.0625 to 0.0625
- leaf_parent: int32 [8], replicated, may hold values from 0 to 1, as said below
- leaf_sizes: int32 [8], replicated, may hold values from 1024 to 2048, as said below
- leaf_map: int32 [8, 16], replicated, may hold values from 0 to 63, as said below
- mid_map: int32 [2, 32], replicated, may hold values from 0 to 79, as said below
Outputs:
- leaf_sol: float32 [8, 2048, 256], P('subtree', 'front')
- mid_sol: float32 [2, 4096, 256], P(None, 'front')
- root_sol: float32 [10240, 256], P('front')
The draws below stay inside these ranges and needn't reach their ends.
Inputs may be any that keep to these rules, and one draw needn't show every extreme that they name: `leaf_parent`: every level-1 front is the parent of at least one lowest-level front. `leaf_sizes`: a multiple of 128; some front has all 2048 rows live. `leaf_map`: a front's blocks go to distinct parent blocks; update block b of a lowest-level front, with c = b // 4, goes to c * 8 + i or to that plus 4096 / 128, for some i with 0 <= i < 8. `mid_map`: a front's blocks go to distinct root blocks; update block b of a level-1 front, with c = b // 8, goes to c * 20 + i for some i with 0 <= i < 20.
All inputs are finite; a program needn't handle non-finite values.
Results may differ from the reference program's by a relative error of at most 0.00013.
Values sent between devices are 32-bit elements; how exact they have to be, the bound alone decides.
No kernel may reach another device: no remote copies, remote signals or barrier semaphores. Data moves between devices by JAX's collectives and lax.ppermute only.
A program may use at most 128 MiB of HBM per device.

```python
import jax
import jax.numpy as jnp
from jax import lax

LEAF_PIV = 2048
MID_PIV = 4096
ROOT_ORD = 10240
BLOCK = 128
SCEN = 256
LEAVES = 8
MIDS = 2
LEAF_SPAN = 4
MID_SPAN = 8
ROOT_SPAN = 20


def draw_leaf_parent(key, part):
    base = jax.random.randint(key, (LEAVES,), 0, MIDS)
    order = jax.random.permutation(jax.random.fold_in(key, 7), LEAVES)
    chosen = order[:MIDS]
    return base.at[chosen].set(jnp.arange(MIDS, dtype=jnp.int32)).astype(jnp.int32)


def draw_leaf_sizes(key, part):
    counts = jax.random.randint(key, (LEAVES,), LEAF_PIV // (2 * BLOCK), LEAF_PIV // BLOCK + 1)
    chosen = jax.random.randint(jax.random.fold_in(key, 3), (), 0, LEAVES)
    counts = counts.at[chosen].set(LEAF_PIV // BLOCK)
    return (counts * BLOCK).astype(jnp.int32)


def draw_leaf_map(key, part):
    columns = LEAF_PIV // BLOCK // LEAF_SPAN
    keys = jax.random.split(key, LEAVES * columns)

    def pick_one(single):
        return jax.random.permutation(single, 2 * MID_SPAN)[:LEAF_SPAN].astype(jnp.int32)
    picks = jax.vmap(pick_one)(keys).reshape(LEAVES, columns, LEAF_SPAN)
    steps_up = jnp.arange(LEAF_SPAN, dtype=jnp.int32)
    picks = picks.at[0, 0].set(steps_up)
    picks = picks.at[LEAVES - 1, columns - 1].set(2 * MID_SPAN - 1 - steps_up)
    halves = picks // MID_SPAN
    within = picks % MID_SPAN
    column = jnp.arange(columns, dtype=jnp.int32)[None, :, None]
    blocks = halves * (MID_PIV // BLOCK) + column * MID_SPAN + within
    return blocks.reshape(LEAVES, LEAF_PIV // BLOCK).astype(jnp.int32)


def draw_mid_map(key, part):
    columns = MID_PIV // BLOCK // MID_SPAN
    keys = jax.random.split(key, MIDS * columns)

    def pick_one(single):
        return jax.random.permutation(single, ROOT_SPAN)[:MID_SPAN].astype(jnp.int32)
    picks = jax.vmap(pick_one)(keys).reshape(MIDS, columns, MID_SPAN)
    steps_up = jnp.arange(MID_SPAN, dtype=jnp.int32)
    picks = picks.at[0, 0].set(steps_up)
    picks = picks.at[MIDS - 1, columns - 1].set(ROOT_SPAN - 1 - steps_up)
    column = jnp.arange(columns, dtype=jnp.int32)[None, :, None]
    blocks = column * ROOT_SPAN + picks
    return blocks.reshape(MIDS, MID_PIV // BLOCK).astype(jnp.int32)


def block_scale(own_key, dims, cuts, low, high):
    def one(position, parts):
        steps = jax.random.uniform(jax.random.fold_in(jax.random.fold_in(own_key, 6), position), (parts,), jnp.float32, low / len(cuts), high / len(cuts))
        return jnp.repeat(jnp.exp(steps), dims[position] // parts).reshape((-1,) + (1,) * (len(dims) - position - 1))

    loudness = one(*cuts[0])
    for cut in cuts[1:]:
        loudness = loudness * one(*cut)
    return loudness


def scatter_about(key, shape, scale, reach, shards=(), kind=jnp.bfloat16):
    level = block_scale(key, shape, shards, -0.22, 0.18) if shards else 1.0
    result = jax.random.normal(key, shape, jnp.float32) * scale * level
    return jnp.minimum(jnp.maximum(result, -reach), reach).astype(kind)


def setup_inputs(seed: int = 0) -> dict:
    arg_keys = jax.random.split(jax.random.key(seed), 18)
    leaf_rhs = scatter_about(arg_keys[0], (LEAVES, LEAF_PIV, SCEN), 1.0, 6.0, ((0, 8), (1, 4)), jnp.float32)
    mid_rhs = scatter_about(arg_keys[1], (MIDS, MID_PIV, SCEN), 1.0, 6.0, ((1, 4),), jnp.float32)
    root_rhs = scatter_about(arg_keys[2], (ROOT_ORD, SCEN), 1.0, 6.0, ((0, 4),), jnp.float32)
    leaf_lower = scatter_about(arg_keys[3], (LEAVES, LEAF_PIV, LEAF_PIV), LEAF_PIV ** -0.5, 0.125, ((0, 8), (2, 4)), jnp.float32)
    leaf_below = scatter_about(arg_keys[4], (LEAVES, LEAF_PIV, LEAF_PIV), LEAF_PIV ** -0.5, 0.125, ((0, 8), (2, 4)), jnp.float32)
    leaf_right = scatter_about(arg_keys[5], (LEAVES, LEAF_PIV, LEAF_PIV), LEAF_PIV ** -0.5, 0.125, ((0, 8), (2, 4)), jnp.float32)
    leaf_upper = scatter_about(arg_keys[6], (LEAVES, LEAF_PIV, LEAF_PIV), LEAF_PIV ** -0.5, 0.125, ((0, 8), (2, 4)), jnp.float32)
    mid_lower = scatter_about(arg_keys[7], (MIDS, MID_PIV, MID_PIV), MID_PIV ** -0.5, 0.09375, ((1, 8), (2, 4)), jnp.float32)
    mid_below = scatter_about(arg_keys[8], (MIDS, MID_PIV, MID_PIV), MID_PIV ** -0.5, 0.09375, ((1, 4), (2, 8)), jnp.float32)
    mid_right = scatter_about(arg_keys[9], (MIDS, MID_PIV, MID_PIV), MID_PIV ** -0.5, 0.09375, ((1, 8), (2, 4)), jnp.float32)
    mid_upper = scatter_about(arg_keys[10], (MIDS, MID_PIV, MID_PIV), MID_PIV ** -0.5, 0.09375, ((1, 4), (2, 8)), jnp.float32)
    root_lower = scatter_about(arg_keys[11], (ROOT_ORD, ROOT_ORD), ROOT_ORD ** -0.5, 0.0625, ((0, 8), (1, 4)), jnp.float32)
    root_upper = scatter_about(arg_keys[12], (ROOT_ORD, ROOT_ORD), ROOT_ORD ** -0.5, 0.0625, ((0, 4), (1, 8)), jnp.float32)
    leaf_parent = draw_leaf_parent(jax.random.fold_in(arg_keys[17], 71), 0)
    leaf_sizes = draw_leaf_sizes(jax.random.fold_in(arg_keys[17], 71), 0)
    leaf_map = draw_leaf_map(jax.random.fold_in(arg_keys[17], 71), 0)
    mid_map = draw_mid_map(jax.random.fold_in(arg_keys[17], 71), 0)
    return {"leaf_rhs": leaf_rhs, "mid_rhs": mid_rhs, "root_rhs": root_rhs, "leaf_lower": leaf_lower, "leaf_below": leaf_below, "leaf_right": leaf_right, "leaf_upper": leaf_upper, "mid_lower": mid_lower, "mid_below": mid_below, "mid_right": mid_right, "mid_upper": mid_upper, "root_lower": root_lower, "root_upper": root_upper, "leaf_parent": leaf_parent, "leaf_sizes": leaf_sizes, "leaf_map": leaf_map, "mid_map": mid_map}


def batched(matrix, vector):
    return jnp.einsum('fab,fbr->far', matrix.astype(jnp.float32), vector.astype(jnp.float32), precision=lax.Precision.HIGHEST)


def reference(leaf_rhs, mid_rhs, root_rhs, leaf_lower, leaf_below, leaf_right, leaf_upper, mid_lower, mid_below, mid_right, mid_upper, root_lower, root_upper, leaf_parent, leaf_sizes, leaf_map, mid_map):
    positions = jnp.arange(LEAF_PIV, dtype=jnp.int32)
    live = (positions[None, :] < leaf_sizes[:, None]).astype(jnp.float32)[:, :, None]
    leaf_fwd = live * batched(leaf_lower, live * leaf_rhs)
    leaf_contrib = -batched(leaf_below, leaf_fwd)
    mid_blocks = 2 * MID_PIV // BLOCK
    mid_front = jnp.zeros((MIDS, mid_blocks, BLOCK, SCEN), jnp.float32)
    mid_front = mid_front.at[leaf_parent[:, None], leaf_map].add(leaf_contrib.reshape(LEAVES, LEAF_PIV // BLOCK, BLOCK, SCEN))
    mid_front = mid_front.reshape(MIDS, 2 * MID_PIV, SCEN)
    mid_fwd = batched(mid_lower, mid_rhs + mid_front[:, :MID_PIV])
    mid_contrib = mid_front[:, MID_PIV:] - batched(mid_below, mid_fwd)
    root_blocks = jnp.zeros((ROOT_ORD // BLOCK, BLOCK, SCEN), jnp.float32)
    root_blocks = root_blocks.at[mid_map].add(mid_contrib.reshape(MIDS, MID_PIV // BLOCK, BLOCK, SCEN))
    root_start = root_rhs + root_blocks.reshape(ROOT_ORD, SCEN)
    root_fwd = jnp.dot(root_lower, root_start, preferred_element_type=jnp.float32, precision=lax.Precision.HIGHEST)
    root_sol = jnp.dot(root_upper, root_fwd, preferred_element_type=jnp.float32, precision=lax.Precision.HIGHEST)
    mid_ext = root_sol.reshape(ROOT_ORD // BLOCK, BLOCK, SCEN)[mid_map].reshape(MIDS, MID_PIV, SCEN)
    mid_sol = batched(mid_upper, mid_fwd - batched(mid_right, mid_ext))
    whole_mid = jnp.concatenate([mid_sol, mid_ext], axis=1).reshape(MIDS, mid_blocks, BLOCK, SCEN)
    leaf_ext = whole_mid[leaf_parent[:, None], leaf_map].reshape(LEAVES, LEAF_PIV, SCEN)
    leaf_sol = live * batched(leaf_upper, live * (leaf_fwd - batched(leaf_right, leaf_ext)))
    return leaf_sol, mid_sol, root_sol
```

```python
import functools

import jax
import jax.numpy as jnp
from jax import lax
from jax.experimental import pallas as pl
from jax.experimental.pallas import tpu as pltpu
from jax.sharding import PartitionSpec as P

F32 = jnp.float32
BF16 = jnp.bfloat16
CHAINS = 1
BLOCK_BYTES = 1 << 21
VMEM_LIMIT = 40 << 20


def partner(x, axis, mask, n):
    return lax.ppermute(x, axis, [(i, i ^ mask) for i in range(n)])


def halving_order(masks):
    if not masks:
        return [0]
    rest = halving_order(masks[1:])
    return [masks[0] ^ c for c in rest] + rest


def pick_rows(rows, depth):
    best = 8
    for d in range(8, rows + 1, 8):
        if rows % d == 0 and d * depth * 4 <= BLOCK_BYTES:
            best = d
    return best


def put(x2, slot, start, value):
    n = value.shape[1]
    rows = pl.ds(start, value.shape[0])
    high = value.astype(BF16)
    x2[slot, rows, pl.ds(0, n)] = high
    x2[slot, rows, pl.ds(n, n)] = (value - high.astype(F32)).astype(BF16)


def product(a, x2):
    n = x2.shape[1] // 2
    high = a.astype(BF16)
    low = (a - high.astype(F32)).astype(BF16)
    both = jnp.dot(high, x2, preferred_element_type=F32)
    return (both[:, :n] + both[:, n:]) + jnp.dot(low, x2[:, :n], preferred_element_type=F32)


def matmul(
    name,
    meta,
    matrix,
    rows,
    width,
    index,
    ins,
    outs,
    slots=1,
    slot_of=None,
    prologue=None,
    extra=(),
    x2=None,
    keep_x2=False,
    scratch=(),
    finish=None,
    sign=1.0,
    in_specs=None,
):
    depth = matrix.shape[2]
    total = sum(outs)
    steps = total // rows
    per = steps // len(outs)
    n_in, n_out, n_extra = len(ins), len(outs), len(extra)
    x2_shape = (slots, depth, 2 * width)
    given = x2 is not None

    def whole(a):
        nd = len(a)
        return pl.BlockSpec(a, lambda i, m, nd=nd: (0,) * nd)

    def kernel(meta_ref, a_ref, *refs):
        i = pl.program_id(0)
        in_refs, refs = refs[:n_in], refs[n_in:]
        if given:
            x2_ref, refs = refs[0], refs[1:]
        out_refs, refs = refs[:n_out], refs[n_out:]
        extra_refs, refs = refs[:n_extra], refs[n_extra:]
        if not given:
            x2_ref, refs = refs[0], refs[1:]

            @pl.when(i == 0)
            def _():
                prologue(meta_ref, in_refs, extra_refs, x2_ref, refs)

        slot = 0 if slot_of is None else slot_of(i)
        acc = product(a_ref[0], x2_ref[slot])
        if sign != 1.0:
            acc = -acc
        for j in range(n_out):

            @pl.when(i // per == j)
            def _():
                start = pl.multiple_of((i - j * per) * rows, rows)
                out_refs[j][pl.ds(start, rows), :] = acc

        if finish is not None:

            @pl.when(i == steps - 1)
            def _():
                finish(meta_ref, in_refs, out_refs)

    out_shape = [jax.ShapeDtypeStruct((r, width), F32) for r in outs]
    out_shape += [jax.ShapeDtypeStruct(e, F32) for e in extra]
    out_specs = [whole(o.shape) for o in out_shape]
    scratch_shapes = list(scratch)
    args = [matrix, *ins]
    specs = [pl.BlockSpec((1, rows, depth), lambda i, m: (*index(i, m), 0))]
    specs += in_specs if in_specs is not None else [whole(a.shape) for a in ins]
    if given:
        args.append(x2)
        specs.append(whole(x2_shape))
    elif keep_x2:
        out_shape.append(jax.ShapeDtypeStruct(x2_shape, BF16))
        out_specs.append(whole(x2_shape))
    else:
        scratch_shapes = [pltpu.VMEM(x2_shape, BF16)] + scratch_shapes
    return pl.pallas_call(
        kernel,
        out_shape=out_shape,
        grid_spec=pltpu.PrefetchScalarGridSpec(
            num_scalar_prefetch=1,
            grid=(steps,),
            in_specs=specs,
            out_specs=out_specs,
            scratch_shapes=scratch_shapes,
        ),
        compiler_params=pltpu.CompilerParams(
            dimension_semantics=("arbitrary",), vmem_limit_bytes=VMEM_LIMIT
        ),
        cost_estimate=pl.CostEstimate(
            flops=6 * total * depth * width,
            bytes_accessed=4 * total * depth,
            transcendentals=0,
        ),
        name=name,
    )(meta, *args)


def solve(
    n_sub,
    n_front,
    tables,
    leaf_rhs,
    mid_rhs,
    root_rhs,
    leaf_lower,
    leaf_below,
    leaf_right,
    leaf_upper,
    mid_lower,
    mid_below,
    mid_right,
    mid_upper,
    root_lower,
    root_upper,
):
    meta0, meta, at = tables
    width = leaf_rhs.shape[1]
    local = leaf_rhs.shape[0]
    fronts, mid_rows = mid_rhs.shape[0], mid_rhs.shape[1]
    root_rows = root_rhs.shape[0]
    block, sub, per_stream = at["block"], at["sub"], at["per_stream"]
    half_leaf = local // 2
    half_fronts = fronts // 2
    mid_width = mid_rows // block
    f_bits = n_front.bit_length() - 1
    z_bits = n_sub.bit_length() - 2
    f_masks = [1 << j for j in range(f_bits)]
    f_masks = [f_masks, f_masks[::-1]]
    z_masks = [2 * ((2 << j) - 1) for j in range(z_bits)]
    z_masks = [z_masks, z_masks[::-1]]
    over_front = lambda x, m: partner(x, "front", m, n_front)
    over_sub = lambda x, m: partner(x, "subtree", m, n_sub)

    def scatter_sum(send, keep, masks):
        for j, m in enumerate(masks):
            got = over_front(send, m)
            if j + 1 == len(masks):
                return keep, got
            h = keep.shape[0] // 2
            send, keep = keep[:h] + got[:h], keep[h:] + got[h:]

    def sum_front(value, masks):
        for m in masks[:-1]:
            value = value + over_front(value, m)
        return value, over_front(value, masks[-1])

    def sum_subtree(send, keep):
        got = over_sub(send, 1)
        h = keep.shape[0] // 2
        mine, other = [], []
        for t in range(2):
            value = keep[t * h : (t + 1) * h] + got[t * h : (t + 1) * h]
            for m in z_masks[t]:
                value = value + over_sub(value, m)
            mine.append(value)
            other.append(over_sub(value, 1))
        return mine, other

    def leaf_phase(name, meta_, matrix, ins, prologue, extra=()):
        half = n_front // 2
        rows = half_leaf
        first = lambda base: (lambda i, m: (0, m[base + i]))
        outs = [half * rows] * 2
        res = matmul(
            name + "_send", meta_, matrix, rows, width, first(at["order"]), ins, outs,
            prologue=prologue, extra=extra, keep_x2=True,
        )
        sends, extras, x2 = res[:2], res[2:-1], res[-1]
        keeps = matmul(
            name + "_keep", meta_, matrix, rows, width, first(at["order"] + n_front), [], outs, x2=x2
        )
        terms = []
        for t in range(2):
            terms += scatter_sum(sends[t], keeps[t], f_masks[t])
        return terms, extras

    def live_rows(m, t, value):
        ids = lax.broadcasted_iota(jnp.int32, value.shape, 0) + t * half_leaf
        return jnp.where(ids < m[at["live"]], value, 0.0)

    def pro(m, ins, extra, x2, _):
        for t in range(2):
            put(x2, 0, t * half_leaf, live_rows(m, t, ins[0][pl.ds(t * half_leaf, half_leaf), :]))

    terms, _ = leaf_phase("leaf_lower", meta0, leaf_lower, [leaf_rhs], pro)

    def pro(m, ins, extra, x2, _):
        for t in range(2):
            fwd = live_rows(m, t, ins[2 * t][...] + ins[2 * t + 1][...])
            extra[0][pl.ds(t * half_leaf, half_leaf), :] = fwd
            put(x2, 0, t * half_leaf, fwd)

    terms, (leaf_fwd,) = leaf_phase("leaf_below", meta0, leaf_below, terms, pro, [(local, width)])
    contrib = [-(terms[2 * t] + terms[2 * t + 1]) for t in range(2)]

    pieces, offsets = [], []
    for t in range(2):
        bufs, offs = [contrib[t]], [0]
        for m in z_masks[t]:
            bufs, offs = bufs + [over_sub(b, m) for b in bufs], offs + [o ^ m for o in offs]
        pieces += bufs
        offsets += [(t, o) for o in offs]

    def assemble(m, *refs):
        ins, out = refs[:-1], refs[-1]
        out[...] = jnp.zeros_like(out)
        for ref, (t, off) in zip(ins, offsets):
            leaf = m[at["self"]] ^ off
            for j in range(per_stream):
                row = m[at["pivot"] + leaf * 2 * per_stream + t * per_stream + j]

                @pl.when(row >= 0)
                def _():
                    rows = pl.ds(pl.multiple_of(row, sub), sub)
                    out[rows, :] += ref[pl.ds(j * sub, sub), :]

    pivot_mine = pl.pallas_call(
        assemble,
        out_shape=jax.ShapeDtypeStruct((fronts * mid_rows, width), F32),
        grid_spec=pltpu.PrefetchScalarGridSpec(
            num_scalar_prefetch=1,
            grid=(1,),
            in_specs=[pl.BlockSpec(p.shape, lambda i, m: (0, 0)) for p in pieces],
            out_specs=pl.BlockSpec((fronts * mid_rows, width), lambda i, m: (0, 0)),
        ),
        compiler_params=pltpu.CompilerParams(vmem_limit_bytes=VMEM_LIMIT),
        name="pivot_rows",
    )(meta, *pieces)
    pivot_other = over_sub(pivot_mine, 1)
    mid_flat = mid_rhs.reshape(fronts * mid_rows, width)

    def front_products(name, matrix, prologue_of, ins_of, specs_of=None, extra_of=None):
        out_rows = matrix.shape[1]
        rows = pick_rows(out_rows, matrix.shape[2])
        steps = out_rows // rows
        results = []
        extras = None
        for t in range(2):
            res = matmul(
                f"{name}_{t}", meta, matrix, rows, width,
                lambda i, m, t=t: (t * half_fronts + i // steps, i % steps),
                ins_of(t, extras), [half_fronts * out_rows],
                slots=half_fronts, slot_of=lambda i: i // steps, prologue=prologue_of(t),
                in_specs=specs_of(t) if specs_of else None,
                extra=extra_of(t) if extra_of else (),
            )
            if len(res) > 1:
                extras = res[1]
            results.append(sum_front(res[0], f_masks[t]))
        return results, extras

    def pro_of(t):
        def pro(m, ins, extra, x2, _):
            for q in range(half_fronts):
                rows = pl.ds(q * mid_rows, mid_rows)
                put(x2, q, 0, ins[0][rows, :] + (ins[1][rows, :] + ins[2][rows, :]))

        return pro

    part = (half_fronts * mid_rows, width)
    mid_fwd, _ = front_products(
        "mid_lower", mid_lower, pro_of, lambda t, e: [mid_flat, pivot_mine, pivot_other],
        specs_of=lambda t: [pl.BlockSpec(part, lambda i, m: (t, 0))] * 3,
    )

    def core_products(name, matrix, prologue_of, ins, finish_of=None, sign=1.0):
        out_rows = matrix.shape[1]
        rows = pick_rows(out_rows, matrix.shape[2])
        steps = out_rows // rows
        results = []
        for flip in (1, 0):
            results += matmul(
                f"{name}_{flip}", meta, matrix, rows, width,
                lambda i, m, flip=flip: ((m[at["core"]] ^ flip) * half_fronts + i // steps, i % steps),
                ins, [half_fronts * out_rows],
                slots=half_fronts, slot_of=lambda i: i // steps, prologue=prologue_of(flip),
                finish=finish_of(flip) if finish_of else None, sign=sign,
            )
        return sum_subtree(*results)

    own_rows = mid_lower.shape[1]

    def pro_of(flip):
        def pro(m, ins, extra, x2, _):
            for t in range(2):

                @pl.when((m[at["core"]] ^ flip) == t)
                def _():
                    for q in range(half_fronts):
                        rows = pl.ds(q * own_rows, own_rows)
                        put(x2, q, 0, ins[2 * t][rows, :] + ins[2 * t + 1][rows, :])

        return pro

    def finish_of(flip):
        def finish(m, ins, outs):
            first = (m[at["core"]] ^ flip) * (half_fronts * mid_rows)
            for u in range(2 * per_stream):
                row = m[at["update"] + u] - first

                @pl.when((row >= 0) & (row < half_fronts * mid_rows))
                def _():
                    rows = pl.ds(pl.multiple_of(row, sub), sub)
                    src = ins[4 + u // per_stream]
                    outs[0][rows, :] += src[pl.ds((u % per_stream) * sub, sub), :]

        return finish

    fwd_terms = [*mid_fwd[0], *mid_fwd[1]]
    mine, other = core_products(
        "mid_below", mid_below, pro_of, fwd_terms + contrib, finish_of, sign=-1.0
    )

    mid_half = half_fronts * mid_rows // 2

    def root_pro(m, ins, extra, x2, scr):
        total = scr[0]
        total[...] = ins[0][...]
        for w in range(2):
            half = m[at["core"]] ^ w
            for t in range(2):
                src = ins[1 + 2 * w + t]
                for k in range(mid_half // block):
                    row = t * mid_half + k * block
                    front = half * half_fronts + row // mid_rows
                    slot = m[at["root"] + front * mid_width + (row % mid_rows) // block]
                    rows = pl.ds(pl.multiple_of(slot * block, block), block)
                    total[rows, :] += src[pl.ds(k * block, block), :]
        put(x2, 0, 0, total[...])

    out_rows = root_lower.shape[0] // 2
    rows = pick_rows(out_rows, root_lower.shape[1])
    steps = out_rows // rows
    matrix = root_lower[None]
    h0, x2 = matmul(
        "root_lower_0", meta, matrix, rows, width, lambda i, m: (0, i),
        [root_rhs, *mine, *other], [out_rows], prologue=root_pro, keep_x2=True,
        scratch=[pltpu.VMEM((root_rows, width), F32)],
    )
    root_fwd = list(sum_front(h0, f_masks[0]))
    (h1,) = matmul(
        "root_lower_1", meta, matrix, rows, width, lambda i, m: (0, steps + i), [], [out_rows], x2=x2
    )
    root_fwd += sum_front(h1, f_masks[1])

    def pro(m, ins, extra, x2, _):
        for t in range(2):
            put(x2, 0, t * out_rows, ins[2 * t][...] + ins[2 * t + 1][...])

    half_root = root_rows // 2
    rows = pick_rows(half_root, root_upper.shape[1])
    steps_up = half_root // rows
    matrix = root_upper[None]
    row_of = lambda flip: (lambda i, m: (0, (m[at["core"]] ^ flip) * steps_up + i))
    send, x2 = matmul(
        "root_upper_1", meta, matrix, rows, width, row_of(1), root_fwd, [half_root],
        prologue=pro, keep_x2=True,
    )
    (keep,) = matmul(
        "root_upper_0", meta, matrix, rows, width, row_of(0), [], [half_root], x2=x2
    )
    mine, other = sum_subtree(send, keep)

    def place(m, ins, out):
        h = ins[0].shape[0]
        for w in range(2):
            for t in range(2):
                start = (m[at["core"]] ^ w) * (2 * h) + t * h
                out[pl.ds(pl.multiple_of(start, h), h), :] = ins[2 * w + t][...]

    def pro_of(t):
        def pro(m, ins, extra, x2, _):
            if t == 0:
                place(m, ins, extra[0])
                root = extra[0]
            else:
                root = ins[0]
            for q in range(half_fronts):
                for k in range(mid_width):
                    slot = m[at["root"] + (t * half_fronts + q) * mid_width + k]
                    rows = pl.ds(pl.multiple_of(slot * block, block), block)
                    put(x2, q, k * block, root[rows, :])

        return pro

    mid_ext, root_sol = front_products(
        "mid_right", mid_right, pro_of, lambda t, e: [*mine, *other] if t == 0 else [e],
        extra_of=lambda t: [(root_rows, width)] if t == 0 else [],
    )
    ext_terms = [*mid_ext[0], *mid_ext[1]]

    def pro_of(flip):
        def pro(m, ins, extra, x2, _):
            for t in range(2):

                @pl.when((m[at["core"]] ^ flip) == t)
                def _():
                    for q in range(half_fronts):
                        rows = pl.ds(q * own_rows, own_rows)
                        a, b, c, d = (ins[j][rows, :] for j in (2 * t, 2 * t + 1, 4 + 2 * t, 5 + 2 * t))
                        put(x2, q, 0, (a + b) - (c + d))

        return pro

    mine, other = core_products("mid_upper", mid_upper, pro_of, fwd_terms + ext_terms)

    def pro(m, ins, extra, x2, _):
        place(m, ins, extra[0])
        for u in range(2 * per_stream):
            rows = pl.ds(pl.multiple_of(m[at["ext_row"] + u], sub), sub)

            @pl.when(m[at["ext_root"] + u] == 0)
            def _():
                put(x2, 0, u * sub, extra[0][rows, :])

            @pl.when(m[at["ext_root"] + u] != 0)
            def _():
                put(x2, 0, u * sub, ins[4][rows, :])

    terms, (mid_sol,) = leaf_phase(
        "leaf_right", meta, leaf_right, [*mine, *other, root_sol], pro,
        [(fronts * mid_rows, width)],
    )

    def pro(m, ins, extra, x2, _):
        for t in range(2):
            back = ins[0][pl.ds(t * half_leaf, half_leaf), :] - (ins[1 + 2 * t][...] + ins[2 + 2 * t][...])
            put(x2, 0, t * half_leaf, live_rows(m, t, back))

    terms, _ = leaf_phase("leaf_upper", meta0, leaf_upper, [leaf_fwd, *terms], pro)
    leaf_sol = jnp.concatenate([terms[0] + terms[1], terms[2] + terms[3]], axis=0)
    ids = jnp.arange(local, dtype=jnp.int32)[:, None]
    leaf_sol = jnp.where(ids < meta0[at["live"]], leaf_sol, 0.0)
    return leaf_sol, mid_sol.reshape(mid_rhs.shape), root_sol


def on_device(
    n_sub,
    n_front,
    leaf_rhs,
    mid_rhs,
    root_rhs,
    leaf_lower,
    leaf_below,
    leaf_right,
    leaf_upper,
    mid_lower,
    mid_below,
    mid_right,
    mid_upper,
    root_lower,
    root_upper,
    leaf_parent,
    leaf_sizes,
    leaf_map,
    mid_map,
):
    group = lax.axis_index("subtree").astype(jnp.int32)
    column = lax.axis_index("front").astype(jnp.int32)
    local = leaf_rhs.shape[1]
    scenarios = leaf_rhs.shape[2]
    block = local * n_front // leaf_map.shape[1]
    mid_rows = mid_rhs.shape[1]
    mid_width = mid_rows // block
    root_width = root_rhs.shape[0] // block
    leaf_width = local // block
    sub = min(block, local // 2)
    per_stream = (local // 2) // sub
    leaves = leaf_map.shape[0]
    f_bits = n_front.bit_length() - 1
    masks = [1 << j for j in range(f_bits)]
    orders = [halving_order(masks), halving_order(masks[::-1])]
    half = n_front // 2
    table = [(o, t) for t in range(2) for o in orders[t][:half]]
    table += [(o, t) for t in range(2) for o in orders[t][half:]]
    order = (column ^ jnp.array([o for o, _ in table], jnp.int32)) * 2
    order = order + jnp.array([t for _, t in table], jnp.int32)
    own_size = lax.dynamic_slice_in_dim(leaf_sizes, group, 1)
    head = jnp.stack([column, group, group & 1, own_size[0] - column * local])
    meta0 = jnp.concatenate([head, order])

    columns = lax.dynamic_slice_in_dim(leaf_map, column * leaf_width, leaf_width, 1)
    starts = [u * sub for u in range(2 * per_stream)]
    blocks = jnp.stack([columns[:, r // block] for r in starts], axis=1)
    inner = jnp.array([r % block for r in starts], jnp.int32)[None]
    halves = n_front * mid_width
    is_update = blocks >= halves
    slot = blocks - jnp.where(is_update, halves, 0) - column * mid_width
    target = leaf_parent[:, None] * mid_rows + slot * block + inner
    pivot = jnp.where(is_update, -1, target)
    update = jnp.where(is_update, target, -(1 << 24))
    root = lax.dynamic_slice_in_dim(mid_map, column * mid_width, mid_width, 1) - column * root_width
    row = lambda a: lax.dynamic_slice_in_dim(a, group, 1, 0)[0]
    own_update, own_slot = row(is_update), row(slot)
    own_parent = row(leaf_parent)
    root_slot = root.reshape(-1)[jnp.clip(own_parent * mid_width + own_slot, 0, root.size - 1)]
    ext_row = jnp.where(own_update, root_slot * block + inner[0], row(target))
    parts = [
        ("pivot", pivot.reshape(-1)),
        ("update", row(update)),
        ("root", root.reshape(-1)),
        ("ext_root", own_update.astype(jnp.int32)),
        ("ext_row", ext_row),
    ]
    at = {"self": 1, "core": 2, "live": 3, "order": 4}
    at |= {"block": block, "sub": sub, "per_stream": per_stream}
    size = meta0.shape[0]
    for key, value in parts:
        at[key] = size
        size += value.shape[0]
    meta = jnp.concatenate([meta0] + [v.astype(jnp.int32) for _, v in parts])

    width = scenarios // CHAINS
    results = []
    for k in range(CHAINS):
        cols = slice(k * width, (k + 1) * width)
        results.append(
            solve(
                n_sub, n_front, (meta0, meta, at),
                leaf_rhs[0][:, cols], mid_rhs[:, :, cols], root_rhs[:, cols],
                leaf_lower, leaf_below, leaf_right, leaf_upper,
                mid_lower, mid_below, mid_right, mid_upper, root_lower, root_upper,
            )
        )
    outs = [jnp.concatenate(r, axis=-1) if CHAINS > 1 else r[0] for r in zip(*results)]
    return outs[0][None], outs[1], outs[2]


def solution(mesh):
    return jax.shard_map(
        functools.partial(on_device, mesh.shape["subtree"], mesh.shape["front"]),
        mesh=mesh,
        in_specs=(
            P("subtree", "front", None),
            P(None, "front", None),
            P("front", None),
            P("subtree", None, "front"),
            P("subtree", None, "front"),
            P("subtree", None, "front"),
            P("subtree", None, "front"),
            P(None, "subtree", "front"),
            P(None, "front", "subtree"),
            P(None, "subtree", "front"),
            P(None, "front", "subtree"),
            P("subtree", "front"),
            P("front", "subtree"),
            P(),
            P(),
            P(),
            P(),
        ),
        out_specs=(P("subtree", "front", None), P(None, "front", None), P("front", None)),
        check_vma=False,
    )
```

```python
import functools

import jax
import jax.numpy as jnp
from jax import lax
from jax.experimental import pallas as pl
from jax.experimental.pallas import tpu as pltpu
from jax.sharding import PartitionSpec as P

F32 = jnp.float32
BF16 = jnp.bfloat16
CHAINS = 1
Z_STREAMS = 2
BLOCK_BYTES = 13 << 18
CUTS = 2
VMEM_LIMIT = 40 << 20


def partner(x, axis, mask, n):
    return lax.ppermute(x, axis, [(i, i ^ mask) for i in range(n)])


def halving_order(masks):
    if not masks:
        return [0]
    rest = halving_order(masks[1:])
    return [masks[0] ^ c for c in rest] + rest


def pick_depth(rows, depth):
    best = depth
    for d in range(128, depth, 128):
        if depth % d == 0 and (rows * d * 4 <= BLOCK_BYTES or d == 128):
            best = d
    if rows * depth * 4 <= BLOCK_BYTES:
        best = depth
    return best


def put(x2, slot, start, value):
    n = value.shape[1]
    rows = pl.ds(start, value.shape[0])
    high = value.astype(BF16)
    x2[slot, rows, pl.ds(0, n)] = high
    x2[slot, rows, pl.ds(n, n)] = (value - high.astype(F32)).astype(BF16)


def product(a, x2):
    n = x2.shape[1] // 2
    high = a.astype(BF16)
    low = (a - high.astype(F32)).astype(BF16)
    both = jnp.dot(high, x2, preferred_element_type=F32)
    return (both[:, :n] + both[:, n:]) + jnp.dot(low, x2[:, :n], preferred_element_type=F32)


def matmul(
    name,
    meta,
    matrix,
    rows,
    groups,
    width,
    index,
    ins,
    prologue=None,
    slots=1,
    extra=(),
    x2=None,
    keep_x2=False,
    scratch=(),
    finish=None,
    sign=1.0,
    in_specs=None,
    blocks=1,
    cuts=1,
    order=None,
):
    depth = matrix.shape[2]
    chunk = pick_depth(rows * blocks, depth)
    steps = depth // chunk
    outs = groups * blocks * cuts if order is None else 1
    piece = rows // cuts
    n_in, n_extra = len(ins), len(extra)
    x2_shape = (slots, depth, 2 * width)
    given = x2 is not None

    def whole(a):
        nd = len(a)
        return pl.BlockSpec(a, lambda g, k, m, nd=nd: (0,) * nd)

    def kernel(meta_ref, *refs):
        g, k = pl.program_id(0), pl.program_id(1)
        a_refs, refs = refs[:blocks], refs[blocks:]
        in_refs, refs = refs[:n_in], refs[n_in:]
        if given:
            x2_ref, refs = refs[0], refs[1:]
        out_refs, refs = refs[:outs], refs[outs:]
        extra_refs, refs = refs[:n_extra], refs[n_extra:]
        if not given:
            x2_ref, refs = refs[0], refs[1:]

            @pl.when((g == 0) & (k == 0))
            def _():
                prologue(meta_ref, in_refs, extra_refs, x2_ref, refs)

        slot = 0 if slots == 1 else g
        part = x2_ref[slot, pl.ds(pl.multiple_of(k * chunk, chunk), chunk), :]
        whole_a = [a[0] for a in a_refs]
        acc = product(whole_a[0] if blocks == 1 else jnp.concatenate(whole_a, axis=0), part)
        if sign != 1.0:
            acc = -acc
        def write(ref, to, value, first):
            ref[to, :] = value if first else ref[to, :] + value

        def store(first):
            if order is not None:
                for start, size, to in order(meta_ref, g):
                    to = pl.ds(pl.multiple_of(to, size), size)
                    write(out_refs[0], to, acc[start : start + size], first)
                return
            for own in range(groups):

                def body():
                    for c in range(blocks * cuts):
                        value = acc[c * piece : (c + 1) * piece]
                        write(out_refs[own * blocks * cuts + c], pl.ds(0, piece), value, first)

                if groups == 1:
                    body()
                else:
                    pl.when(g == own)(body)

        if steps == 1:
            store(True)
        else:
            pl.when(k == 0)(lambda: store(True))
            pl.when(k != 0)(lambda: store(False))

        if finish is not None:

            @pl.when((g == groups - 1) & (k == steps - 1))
            def _():
                finish(meta_ref, in_refs, out_refs)

    out_rows = piece if order is None else groups * rows
    out_shape = [jax.ShapeDtypeStruct((out_rows, width), F32)] * outs
    out_shape += [jax.ShapeDtypeStruct(e, F32) for e in extra]
    out_specs = [whole(o.shape) for o in out_shape]
    scratch_shapes = list(scratch)
    args = [matrix] * blocks + list(ins)
    specs = [
        pl.BlockSpec((1, rows, chunk), lambda g, k, m, q=q: (*index(q if groups == 1 else g, m), k))
        for q in range(blocks)
    ]
    specs += in_specs if in_specs is not None else [whole(a.shape) for a in ins]
    if given:
        args.append(x2)
        specs.append(whole(x2_shape))
    elif keep_x2:
        out_shape.append(jax.ShapeDtypeStruct(x2_shape, BF16))
        out_specs.append(whole(x2_shape))
    else:
        scratch_shapes = [pltpu.VMEM(x2_shape, BF16)] + scratch_shapes
    return pl.pallas_call(
        kernel,
        out_shape=out_shape,
        grid_spec=pltpu.PrefetchScalarGridSpec(
            num_scalar_prefetch=1,
            grid=(groups, steps),
            in_specs=specs,
            out_specs=out_specs,
            scratch_shapes=scratch_shapes,
        ),
        compiler_params=pltpu.CompilerParams(
            dimension_semantics=("arbitrary", "arbitrary"), vmem_limit_bytes=VMEM_LIMIT
        ),
        cost_estimate=pl.CostEstimate(
            flops=6 * groups * blocks * rows * depth * width,
            bytes_accessed=4 * groups * blocks * rows * depth,
            transcendentals=0,
        ),
        name=name,
    )(meta, *args)


def solve(
    n_sub,
    n_front,
    tables,
    leaf_rhs,
    mid_rhs,
    root_rhs,
    leaf_lower,
    leaf_below,
    leaf_right,
    leaf_upper,
    mid_lower,
    mid_below,
    mid_right,
    mid_upper,
    root_lower,
    root_upper,
):
    meta0, meta, at = tables
    width = leaf_rhs.shape[1]
    local = leaf_rhs.shape[0]
    fronts, mid_rows = mid_rhs.shape[0], mid_rhs.shape[1]
    root_rows = root_rhs.shape[0]
    block, sub, per_stream = at["block"], at["sub"], at["per_stream"]
    half_leaf = local // 2
    half_fronts = fronts // 2
    mid_width = mid_rows // block
    f_bits = n_front.bit_length() - 1
    z_bits = n_sub.bit_length() - 2
    f_masks = [1 << j for j in range(f_bits)]
    f_masks = [f_masks, f_masks[::-1]]
    z_masks = [2 << j for j in range(z_bits)]
    over_front = lambda x, m: partner(x, "front", m, n_front)
    over_sub = lambda x, m: partner(x, "subtree", m, n_sub)

    def scatter_sum(blocks, masks):
        terms = [[b] for b in blocks]
        for m in masks:
            h = len(terms) // 2
            got = [over_front(sum(b), m) for b in terms[:h]]
            terms = [keep + [g] for keep, g in zip(terms[h:], got)]
        return terms[0]

    def sum_front(values, masks):
        terms = []
        for value in values:
            for m in masks[:-1]:
                value = value + over_front(value, m)
            terms += [value, over_front(value, masks[-1])]
        return terms

    top = z_bits - 1
    n_pieces = Z_STREAMS << top

    def sum_subtree(send, keep):
        got = over_sub(send, 1)
        h = keep.shape[0] // Z_STREAMS
        mine, other = [], []
        for t in range(Z_STREAMS):
            parts = [keep[t * h : (t + 1) * h], got[t * h : (t + 1) * h]]
            for j in range(top):
                n = parts[0].shape[0] // 2
                leave = sum(x[:n] for x in parts)
                parts = [sum(x[n:] for x in parts), over_sub(leave, z_masks[j])]
            value = sum(parts)
            value = value + over_sub(value, z_masks[top])
            pieces = [value]
            for j in reversed(range(top)):
                pieces += [over_sub(p, z_masks[j]) for p in pieces]
            mine += pieces
            other += [over_sub(p, 1) for p in pieces]
        return mine, other

    def leave_first(groups, rows):
        per = n_pieces // groups
        size = rows // per

        def order(m, g):
            return [(p * size, size, ((g * per + p) ^ m[at["flip"]]) * size) for p in range(per)]

        return order

    piece_bits = [0]
    for j in reversed(range(top)):
        piece_bits += [o | (1 << j) for o in piece_bits]

    def piece_starts(m, half_rows):
        stream = half_rows // Z_STREAMS
        for w in range(2):
            for t in range(Z_STREAMS):
                for n, off in enumerate(piece_bits):
                    z = (m[at["self"]] // 2) ^ off
                    start = (m[at["core"]] ^ w) * half_rows + t * stream
                    for j in range(top):
                        start = start + ((z >> j) & 1) * (stream >> (j + 1))
                    yield (w * Z_STREAMS + t) * len(piece_bits) + n, start

    def leaf_phase(name, meta_, matrix, ins, prologue, extra=()):
        early = max(n_front // 4, 1)
        spots = [[t * n_front + n for n in range(n_front)] for t in range(2)]
        calls = [spots[0][:early] + spots[1][:early], spots[0][early:] + spots[1][early:]]
        made, extras, x2 = {}, (), None
        for call, chosen in enumerate(calls):

            def pick(q, m, chosen=chosen):
                return 0, m[at["order"] + chosen[q]]

            res = matmul(
                f"{name}_{call}", meta_, matrix, half_leaf, 1, width, pick,
                ins if call == 0 else [], prologue=prologue, blocks=len(chosen),
                extra=extra if call == 0 else (), keep_x2=call == 0, x2=x2,
            )
            made.update(zip(chosen, res))
            if call == 0:
                extras, x2 = res[len(chosen) : -1], res[-1]
        terms = [scatter_sum([made[n] for n in spots[t]], f_masks[t]) for t in range(2)]
        return terms, extras

    def live_rows(m, t, value):
        ids = lax.broadcasted_iota(jnp.int32, value.shape, 0) + t * half_leaf
        return jnp.where(ids < m[at["live"]], value, 0.0)

    def pro(m, ins, extra, x2, _):
        for t in range(2):
            put(x2, 0, t * half_leaf, live_rows(m, t, ins[0][pl.ds(t * half_leaf, half_leaf), :]))

    terms, _ = leaf_phase("leaf_lower", meta0, leaf_lower, [leaf_rhs], pro)

    n_terms = f_bits + 1

    def total_of(refs, t, skip=0):
        return sum(r[...] for r in refs[skip + t * n_terms : skip + (t + 1) * n_terms])

    def pro(m, ins, extra, x2, _):
        for t in range(2):
            fwd = live_rows(m, t, total_of(ins, t))
            extra[0][pl.ds(t * half_leaf, half_leaf), :] = fwd
            put(x2, 0, t * half_leaf, fwd)

    terms, (leaf_fwd,) = leaf_phase("leaf_below", meta0, leaf_below, terms[0] + terms[1], pro, [(local, width)])
    contrib = [-sum(terms[t]) for t in range(2)]

    pieces, offsets = [], []
    for t in range(2):
        bufs, offs = [contrib[t]], [0]
        for m in reversed(z_masks):
            bufs, offs = bufs + [over_sub(b, m) for b in bufs], offs + [o ^ m for o in offs]
        pieces += bufs
        offsets += [(t, o) for o in offs]

    def assemble(m, *refs):
        ins, out = refs[:-1], refs[-1]
        out[...] = jnp.zeros_like(out)
        for ref, (t, off) in zip(ins, offsets):
            leaf = m[at["self"]] ^ off
            for j in range(per_stream):
                row = m[at["pivot"] + leaf * 2 * per_stream + t * per_stream + j]

                @pl.when(row >= 0)
                def _():
                    rows = pl.ds(pl.multiple_of(row, sub), sub)
                    out[rows, :] += ref[pl.ds(j * sub, sub), :]

    pivot_mine = pl.pallas_call(
        assemble,
        out_shape=jax.ShapeDtypeStruct((fronts * mid_rows, width), F32),
        grid_spec=pltpu.PrefetchScalarGridSpec(
            num_scalar_prefetch=1,
            grid=(1,),
            in_specs=[pl.BlockSpec(p.shape, lambda i, m: (0, 0)) for p in pieces],
            out_specs=pl.BlockSpec((fronts * mid_rows, width), lambda i, m: (0, 0)),
        ),
        compiler_params=pltpu.CompilerParams(vmem_limit_bytes=VMEM_LIMIT),
        name="pivot_rows",
    )(meta, *pieces)
    pivot_other = over_sub(pivot_mine, 1)
    mid_flat = mid_rhs.reshape(fronts * mid_rows, width)

    def front_products(name, matrix, prologue_of, ins_of, specs_of=None, extra_of=None):
        results = []
        extras = None
        for t in range(2):
            res = matmul(
                f"{name}_{t}", meta, matrix, matrix.shape[1], half_fronts, width,
                lambda g, m, t=t: (t * half_fronts + g, 0), ins_of(t, extras),
                prologue=prologue_of(t), slots=half_fronts,
                in_specs=specs_of(t) if specs_of else None,
                extra=extra_of(t) if extra_of else (), cuts=CUTS,
            )
            n_parts = half_fronts * CUTS
            if len(res) > n_parts:
                extras = res[n_parts]
            results.append(sum_front(res[:n_parts], f_masks[t]))
        return results, extras

    def pro_of(t):
        def pro(m, ins, extra, x2, _):
            for q in range(half_fronts):
                rows = pl.ds(q * mid_rows, mid_rows)
                put(x2, q, 0, ins[0][rows, :] + (ins[1][rows, :] + ins[2][rows, :]))

        return pro

    part = (half_fronts * mid_rows, width)
    mid_fwd, _ = front_products(
        "mid_lower", mid_lower, pro_of, lambda t, e: [mid_flat, pivot_mine, pivot_other],
        specs_of=lambda t: [pl.BlockSpec(part, lambda g, k, m: (t, 0))] * 3,
    )

    def core_products(name, matrix, prologue_of, ins, finish_of=None, sign=1.0):
        results = []
        for flip in (1, 0):
            results += matmul(
                f"{name}_{flip}", meta, matrix, matrix.shape[1], half_fronts, width,
                lambda g, m, flip=flip: ((m[at["core"]] ^ flip) * half_fronts + g, 0), ins,
                prologue=prologue_of(flip), slots=half_fronts, sign=sign,
                finish=finish_of(flip) if finish_of else None,
                order=leave_first(half_fronts, matrix.shape[1]),
            )
        return sum_subtree(*results)

    own_rows = mid_lower.shape[1]
    n_parts = half_fronts * CUTS

    def pro_of(flip):
        def pro(m, ins, extra, x2, _):
            for t in range(2):

                @pl.when((m[at["core"]] ^ flip) == t)
                def _():
                    for n in range(n_parts):
                        value = ins[2 * (t * n_parts + n)][...] + ins[2 * (t * n_parts + n) + 1][...]
                        put(x2, n // CUTS, n % CUTS * (own_rows // CUTS), value)

        return pro

    def finish_of(flip):
        def finish(m, ins, outs):
            first = (m[at["core"]] ^ flip) * (half_fronts * mid_rows)
            for u in range(2 * per_stream):
                row = m[at["update"] + u] - first

                @pl.when((row >= 0) & (row < half_fronts * mid_rows))
                def _():
                    size = half_fronts * mid_rows // n_pieces
                    to = ((row // size) ^ m[at["flip"]]) * size + row % size
                    rows = pl.ds(pl.multiple_of(to, sub), sub)
                    src = ins[4 * n_parts + u // per_stream]
                    outs[0][rows, :] += src[pl.ds((u % per_stream) * sub, sub), :]

        return finish

    fwd_terms = [*mid_fwd[0], *mid_fwd[1]]
    mine, other = core_products(
        "mid_below", mid_below, pro_of, fwd_terms + contrib, finish_of, sign=-1.0
    )

    def root_pro(m, ins, extra, x2, scr):
        total = scr[0]
        total[...] = ins[0][...]
        for n, start in piece_starts(m, half_fronts * mid_rows):
            src = ins[1 + n]
            for k in range(src.shape[0] // block):
                slot = m[at["root"] + start // block + k]
                rows = pl.ds(pl.multiple_of(slot * block, block), block)
                total[rows, :] += src[pl.ds(k * block, block), :]
        put(x2, 0, 0, total[...])

    out_rows = root_lower.shape[0] // 2
    matrix = root_lower[None]
    *h0, x2 = matmul(
        "root_lower_0", meta, matrix, out_rows, 1, width, lambda g, m: (0, 0),
        [root_rhs, *mine, *other], prologue=root_pro, keep_x2=True,
        scratch=[pltpu.VMEM((root_rows, width), F32)], cuts=CUTS,
    )
    root_fwd = sum_front(h0, f_masks[0])
    h1 = matmul(
        "root_lower_1", meta, matrix, out_rows, 1, width, lambda g, m: (0, 1), [], x2=x2,
        cuts=CUTS,
    )
    root_fwd += sum_front(h1, f_masks[1])

    def pro(m, ins, extra, x2, _):
        for n in range(2 * CUTS):
            put(x2, 0, n * (out_rows // CUTS), ins[2 * n][...] + ins[2 * n + 1][...])

    half_root = root_rows // 2
    matrix = root_upper[None]
    row_of = lambda flip: (lambda g, m: (0, m[at["core"]] ^ flip))
    send, x2 = matmul(
        "root_upper_1", meta, matrix, half_root, 1, width, row_of(1), root_fwd,
        prologue=pro, keep_x2=True, order=leave_first(1, half_root),
    )
    (keep,) = matmul(
        "root_upper_0", meta, matrix, half_root, 1, width, row_of(0), [], x2=x2,
        order=leave_first(1, half_root),
    )
    mine, other = sum_subtree(send, keep)

    def place(m, ins, out):
        for n, start in piece_starts(m, out.shape[0] // 2):
            h = ins[n].shape[0]
            out[pl.ds(pl.multiple_of(start, h), h), :] = ins[n][...]

    def pro_of(t):
        def pro(m, ins, extra, x2, _):
            if t == 0:
                place(m, ins, extra[0])
                root = extra[0]
            else:
                root = ins[0]
            for q in range(half_fronts):
                for k in range(mid_width):
                    slot = m[at["root"] + (t * half_fronts + q) * mid_width + k]
                    rows = pl.ds(pl.multiple_of(slot * block, block), block)
                    put(x2, q, k * block, root[rows, :])

        return pro

    mid_ext, root_sol = front_products(
        "mid_right", mid_right, pro_of, lambda t, e: [*mine, *other] if t == 0 else [e],
        extra_of=lambda t: [(root_rows, width)] if t == 0 else [],
    )
    ext_terms = [*mid_ext[0], *mid_ext[1]]

    def pro_of(flip):
        def pro(m, ins, extra, x2, _):
            for t in range(2):

                @pl.when((m[at["core"]] ^ flip) == t)
                def _():
                    for n in range(n_parts):
                        k = 2 * (t * n_parts + n)
                        a, b, c, d = (ins[j][...] for j in (k, k + 1, 4 * n_parts + k, 4 * n_parts + k + 1))
                        put(x2, n // CUTS, n % CUTS * (own_rows // CUTS), (a + b) - (c + d))

        return pro

    mine, other = core_products("mid_upper", mid_upper, pro_of, fwd_terms + ext_terms)

    def pro(m, ins, extra, x2, _):
        place(m, ins, extra[0])
        for u in range(2 * per_stream):
            rows = pl.ds(pl.multiple_of(m[at["ext_row"] + u], sub), sub)

            @pl.when(m[at["ext_root"] + u] == 0)
            def _():
                put(x2, 0, u * sub, extra[0][rows, :])

            @pl.when(m[at["ext_root"] + u] != 0)
            def _():
                put(x2, 0, u * sub, ins[-1][rows, :])

    terms, (mid_sol,) = leaf_phase(
        "leaf_right", meta, leaf_right, [*mine, *other, root_sol], pro,
        [(fronts * mid_rows, width)],
    )

    def pro(m, ins, extra, x2, _):
        for t in range(2):
            back = ins[0][pl.ds(t * half_leaf, half_leaf), :] - total_of(ins, t, 1)
            put(x2, 0, t * half_leaf, live_rows(m, t, back))

    terms, _ = leaf_phase("leaf_upper", meta0, leaf_upper, [leaf_fwd, *terms[0], *terms[1]], pro)
    leaf_sol = jnp.concatenate([sum(terms[0]), sum(terms[1])], axis=0)
    ids = jnp.arange(local, dtype=jnp.int32)[:, None]
    leaf_sol = jnp.where(ids < meta0[at["live"]], leaf_sol, 0.0)
    return leaf_sol, mid_sol.reshape(mid_rhs.shape), root_sol


def on_device(
    n_sub,
    n_front,
    leaf_rhs,
    mid_rhs,
    root_rhs,
    leaf_lower,
    leaf_below,
    leaf_right,
    leaf_upper,
    mid_lower,
    mid_below,
    mid_right,
    mid_upper,
    root_lower,
    root_upper,
    leaf_parent,
    leaf_sizes,
    leaf_map,
    mid_map,
):
    group = lax.axis_index("subtree").astype(jnp.int32)
    column = lax.axis_index("front").astype(jnp.int32)
    local = leaf_rhs.shape[1]
    scenarios = leaf_rhs.shape[2]
    block = local * n_front // leaf_map.shape[1]
    mid_rows = mid_rhs.shape[1]
    mid_width = mid_rows // block
    root_width = root_rhs.shape[0] // block
    leaf_width = local // block
    sub = min(block, local // 2)
    per_stream = (local // 2) // sub
    leaves = leaf_map.shape[0]
    f_bits = n_front.bit_length() - 1
    masks = [1 << j for j in range(f_bits)]
    orders = [halving_order(masks), halving_order(masks[::-1])]
    table = [(o, t) for t in range(2) for o in orders[t]]
    order = (column ^ jnp.array([o for o, _ in table], jnp.int32)) * 2
    order = order + jnp.array([t for _, t in table], jnp.int32)
    own_size = lax.dynamic_slice_in_dim(leaf_sizes, group, 1)
    top = n_sub.bit_length() - 3
    flip = (1 << top) - 1
    for j in range(top):
        flip = flip ^ (((group >> (j + 1)) & 1) << (top - 1 - j))
    head = jnp.stack([column, group, group & 1, own_size[0] - column * local, jnp.int32(flip)])
    meta0 = jnp.concatenate([head, order])

    columns = lax.dynamic_slice_in_dim(leaf_map, column * leaf_width, leaf_width, 1)
    starts = [u * sub for u in range(2 * per_stream)]
    blocks = jnp.stack([columns[:, r // block] for r in starts], axis=1)
    inner = jnp.array([r % block for r in starts], jnp.int32)[None]
    halves = n_front * mid_width
    is_update = blocks >= halves
    slot = blocks - jnp.where(is_update, halves, 0) - column * mid_width
    target = leaf_parent[:, None] * mid_rows + slot * block + inner
    pivot = jnp.where(is_update, -1, target)
    update = jnp.where(is_update, target, -(1 << 24))
    root = lax.dynamic_slice_in_dim(mid_map, column * mid_width, mid_width, 1) - column * root_width
    row = lambda a: lax.dynamic_slice_in_dim(a, group, 1, 0)[0]
    own_update, own_slot = row(is_update), row(slot)
    own_parent = row(leaf_parent)
    root_slot = root.reshape(-1)[jnp.clip(own_parent * mid_width + own_slot, 0, root.size - 1)]
    ext_row = jnp.where(own_update, root_slot * block + inner[0], row(target))
    parts = [
        ("pivot", pivot.reshape(-1)),
        ("update", row(update)),
        ("root", root.reshape(-1)),
        ("ext_root", own_update.astype(jnp.int32)),
        ("ext_row", ext_row),
    ]
    at = {"self": 1, "core": 2, "live": 3, "flip": 4, "order": 5}
    at |= {"block": block, "sub": sub, "per_stream": per_stream}
    size = meta0.shape[0]
    for key, value in parts:
        at[key] = size
        size += value.shape[0]
    meta = jnp.concatenate([meta0] + [v.astype(jnp.int32) for _, v in parts])

    width = scenarios // CHAINS
    results = []
    for k in range(CHAINS):
        cols = slice(k * width, (k + 1) * width)
        results.append(
            solve(
                n_sub, n_front, (meta0, meta, at),
                leaf_rhs[0][:, cols], mid_rhs[:, :, cols], root_rhs[:, cols],
                leaf_lower, leaf_below, leaf_right, leaf_upper,
                mid_lower, mid_below, mid_right, mid_upper, root_lower, root_upper,
            )
        )
    outs = [jnp.concatenate(r, axis=-1) if CHAINS > 1 else r[0] for r in zip(*results)]
    return outs[0][None], outs[1], outs[2]


def solution(mesh):
    return jax.shard_map(
        functools.partial(on_device, mesh.shape["subtree"], mesh.shape["front"]),
        mesh=mesh,
        in_specs=(
            P("subtree", "front", None),
            P(None, "front", None),
            P("front", None),
            P("subtree", None, "front"),
            P("subtree", None, "front"),
            P("subtree", None, "front"),
            P("subtree", None, "front"),
            P(None, "subtree", "front"),
            P(None, "front", "subtree"),
            P(None, "subtree", "front"),
            P(None, "front", "subtree"),
            P("subtree", "front"),
            P("front", "subtree"),
            P(),
            P(),
            P(),
            P(),
        ),
        out_specs=(P("subtree", "front", None), P(None, "front", None), P("front", None)),
        check_vma=False,
    )
```

```python
import functools

import jax
import jax.numpy as jnp
from jax import lax
from jax.experimental import pallas as pl
from jax.experimental.pallas import tpu as pltpu
from jax.sharding import PartitionSpec as P

F32 = jnp.float32
BF16 = jnp.bfloat16
CHAINS = 2
Z_STREAMS = 1
BLOCK_BYTES = 1 << 24
CUTS = 1
VMEM_LIMIT = 22 << 20


def partner(x, axis, mask, n):
    return lax.ppermute(x, axis, [(i, i ^ mask) for i in range(n)])


def halving_order(masks):
    if not masks:
        return [0]
    rest = halving_order(masks[1:])
    return [masks[0] ^ c for c in rest] + rest


def pick_depth(rows, depth):
    best = depth
    for d in range(128, depth, 128):
        if depth % d == 0 and (rows * d * 4 <= BLOCK_BYTES or d == 128):
            best = d
    if rows * depth * 4 <= BLOCK_BYTES:
        best = depth
    return best


def put(x2, slot, start, value):
    n = value.shape[1]
    rows = pl.ds(start, value.shape[0])
    high = value.astype(BF16)
    x2[slot, rows, pl.ds(0, n)] = high
    x2[slot, rows, pl.ds(n, n)] = (value - high.astype(F32)).astype(BF16)


def product(a, x2):
    n = x2.shape[1] // 2
    high = a.astype(BF16)
    low = (a - high.astype(F32)).astype(BF16)
    both = jnp.dot(high, x2, preferred_element_type=F32)
    return (both[:, :n] + both[:, n:]) + jnp.dot(low, x2[:, :n], preferred_element_type=F32)


def matmul(
    meta,
    matrix,
    rows,
    groups,
    width,
    index,
    ins,
    prologue=None,
    slots=1,
    extra=(),
    x2=None,
    keep_x2=False,
    scratch=(),
    finish=None,
    sign=1.0,
    in_specs=None,
    blocks=1,
    cuts=1,
    order=None,
    stay=False,
):
    depth = matrix.shape[2]
    chunk = pick_depth(rows * blocks, depth)
    steps = depth // chunk
    outs = groups * blocks * cuts if order is None else 1
    piece = rows // cuts
    n_in, n_extra = len(ins), len(extra)
    x2_shape = (slots, depth, 2 * width)
    given = x2 is not None

    def whole(a):
        nd = len(a)
        return pl.BlockSpec(a, lambda g, k, m, nd=nd: (0,) * nd)

    def kernel(meta_ref, *refs):
        g, k = pl.program_id(0), pl.program_id(1)
        a_refs, refs = refs[:blocks], refs[blocks:]
        in_refs, refs = refs[:n_in], refs[n_in:]
        if given:
            x2_ref, refs = refs[0], refs[1:]
        out_refs, refs = refs[:outs], refs[outs:]
        extra_refs, refs = refs[:n_extra], refs[n_extra:]
        if not given:
            x2_ref, refs = refs[0], refs[1:]

            @pl.when((g == 0) & (k == 0))
            def _():
                prologue(meta_ref, in_refs, extra_refs, x2_ref, refs)

        slot = 0 if slots == 1 else g
        part = x2_ref[slot, pl.ds(pl.multiple_of(k * chunk, chunk), chunk), :]
        whole_a = [a[0] for a in a_refs]
        acc = product(whole_a[0] if blocks == 1 else jnp.concatenate(whole_a, axis=0), part)
        if sign != 1.0:
            acc = -acc

        def write(ref, to, value, first):
            ref[to, :] = value if first else ref[to, :] + value

        def store(first):
            if order is not None:
                for start, size, to in order(meta_ref, g):
                    to = pl.ds(pl.multiple_of(to, size), size)
                    write(out_refs[0], to, acc[start : start + size], first)
                return
            for own in range(groups):

                def body():
                    for c in range(blocks * cuts):
                        value = acc[c * piece : (c + 1) * piece]
                        write(out_refs[own * blocks * cuts + c], pl.ds(0, piece), value, first)

                if groups == 1:
                    body()
                else:
                    pl.when(g == own)(body)

        if steps == 1:
            store(True)
        else:
            pl.when(k == 0)(lambda: store(True))
            pl.when(k != 0)(lambda: store(False))

        if finish is not None:

            @pl.when((g == groups - 1) & (k == steps - 1))
            def _():
                finish(meta_ref, in_refs, out_refs)

    out_rows = piece if order is None else groups * rows
    out_shape = [jax.ShapeDtypeStruct((out_rows, width), F32)] * outs
    out_shape += [jax.ShapeDtypeStruct(e, F32) for e in extra]
    out_specs = [whole(o.shape) for o in out_shape]
    scratch_shapes = list(scratch)
    if stay:
        matrix = pltpu.with_memory_space_constraint(matrix, pltpu.HBM)
    args = [matrix] * blocks + list(ins)
    specs = [
        pl.BlockSpec((1, rows, chunk), lambda g, k, m, q=q: (*index(q if groups == 1 else g, m), k))
        for q in range(blocks)
    ]
    specs += in_specs if in_specs is not None else [whole(a.shape) for a in ins]
    if given:
        args.append(x2)
        specs.append(whole(x2_shape))
    elif keep_x2:
        out_shape.append(jax.ShapeDtypeStruct(x2_shape, BF16))
        out_specs.append(whole(x2_shape))
    else:
        scratch_shapes = [pltpu.VMEM(x2_shape, BF16)] + scratch_shapes
    return pl.pallas_call(
        kernel,
        out_shape=out_shape,
        grid_spec=pltpu.PrefetchScalarGridSpec(
            num_scalar_prefetch=1,
            grid=(groups, steps),
            in_specs=specs,
            out_specs=out_specs,
            scratch_shapes=scratch_shapes,
        ),
        compiler_params=pltpu.CompilerParams(
            dimension_semantics=("arbitrary", "arbitrary"), vmem_limit_bytes=VMEM_LIMIT
        ),
        cost_estimate=pl.CostEstimate(
            flops=6 * groups * blocks * rows * depth * width,
            bytes_accessed=4 * groups * blocks * rows * depth,
            transcendentals=0,
        ),
    )(meta, *args)


def solve(
    gate,
    n_sub,
    n_front,
    tables,
    leaf_rhs,
    mid_rhs,
    root_rhs,
    leaf_lower,
    leaf_below,
    leaf_right,
    leaf_upper,
    mid_lower,
    mid_below,
    mid_right,
    mid_upper,
    root_lower,
    root_upper,
):
    meta0, meta, at = tables
    if gate:
        leaf_rhs = lax.optimization_barrier((leaf_rhs, gate[0]))[0]
    width = leaf_rhs.shape[1]
    local = leaf_rhs.shape[0]
    fronts, mid_rows = mid_rhs.shape[0], mid_rhs.shape[1]
    root_rows = root_rhs.shape[0]
    block, sub, per_stream = at["block"], at["sub"], at["per_stream"]
    half_leaf = local // 2
    half_fronts = fronts // 2
    mid_width = mid_rows // block
    f_bits = n_front.bit_length() - 1
    z_bits = n_sub.bit_length() - 2
    f_masks = [1 << j for j in range(f_bits)]
    f_masks = [f_masks, f_masks[::-1]]
    z_masks = [2 << j for j in range(z_bits)]
    over_front = lambda x, m: partner(x, "front", m, n_front)
    over_sub = lambda x, m: partner(x, "subtree", m, n_sub)

    def scatter_sum(blocks, masks):
        terms = [[b] for b in blocks]
        for m in masks:
            h = len(terms) // 2
            got = [over_front(sum(b), m) for b in terms[:h]]
            terms = [keep + [g] for keep, g in zip(terms[h:], got)]
        return terms[0]

    def sum_front(values, masks):
        terms = []
        for value in values:
            for m in masks[:-1]:
                got = over_front(value, m)
                value = value + got
            terms += [value, over_front(value, masks[-1])]
        return terms

    top = z_bits - 1
    n_pieces = Z_STREAMS << top

    def sum_subtree(sends, keeps):
        got = [over_sub(x, 1) for x in sends]
        mine, other = [], []
        for t in range(Z_STREAMS):
            if len(keeps) == Z_STREAMS:
                parts = [keeps[t], got[t]]
            else:
                h = keeps[0].shape[0] // Z_STREAMS
                parts = [x[0][t * h : (t + 1) * h] for x in (keeps, got)]
            for j in range(top):
                n = parts[0].shape[0] // 2
                leave = sum(x[:n] for x in parts)
                got_low = over_sub(leave, z_masks[j])
                parts = [sum(x[n:] for x in parts), got_low]
            value = sum(parts)
            crossed = over_sub(value, z_masks[top])
            pieces = [value + crossed]
            for j in reversed(range(top)):
                pieces += [over_sub(p, z_masks[j]) for p in pieces]
            mine += pieces
            other += [over_sub(p, 1) for p in pieces]
        return mine, other

    def leave_first(groups, rows, pieces=n_pieces):
        per = pieces // groups
        size = rows // per

        def order(m, g):
            return [(p * size, size, ((g * per + p) ^ m[at["flip"]]) * size) for p in range(per)]

        return order

    piece_bits = [0]
    for j in reversed(range(top)):
        piece_bits += [o | (1 << j) for o in piece_bits]

    def piece_starts(m, half_rows):
        stream = half_rows // Z_STREAMS
        for w in range(2):
            for t in range(Z_STREAMS):
                for n, off in enumerate(piece_bits):
                    z = (m[at["self"]] // 2) ^ off
                    start = (m[at["core"]] ^ w) * half_rows + t * stream
                    for j in range(top):
                        start = start + ((z >> j) & 1) * (stream >> (j + 1))
                    yield (w * Z_STREAMS + t) * len(piece_bits) + n, start

    def leaf_phase(meta_, matrix, ins, prologue, extra=(), stay=False):
        early = max(n_front // 4, 1)
        spots = [[t * n_front + n for n in range(n_front)] for t in range(2)]
        calls = [spots[0][:early] + spots[1][:early], spots[0][early:] + spots[1][early:]]
        made, extras, x2 = {}, (), None
        for call, chosen in enumerate(calls):

            def pick(q, m, chosen=chosen):
                return 0, m[at["order"] + chosen[q]]

            res = matmul(
                meta_, matrix, half_leaf, 1, width, pick,
                ins if call == 0 else [], prologue=prologue, blocks=len(chosen),
                extra=extra if call == 0 else (), keep_x2=call == 0, x2=x2,
                stay=stay and call == 0,
            )
            made.update(zip(chosen, res))
            if call == 0:
                extras, x2 = res[len(chosen) : -1], res[-1]
        terms = [scatter_sum([made[n] for n in spots[t]], f_masks[t]) for t in range(2)]
        return terms, extras

    def live_rows(m, t, value):
        ids = lax.broadcasted_iota(jnp.int32, value.shape, 0) + t * half_leaf
        return jnp.where(ids < m[at["live"]], value, 0.0)

    def pro(m, ins, extra, x2, _):
        for t in range(2):
            put(x2, 0, t * half_leaf, live_rows(m, t, ins[0][pl.ds(t * half_leaf, half_leaf), :]))

    terms, _ = leaf_phase(meta0, leaf_lower, [leaf_rhs], pro, stay=False)

    n_terms = f_bits + 1

    def total_of(refs, t, skip=0):
        return sum(r[...] for r in refs[skip + t * n_terms : skip + (t + 1) * n_terms])

    gate.append(terms[0][-1])

    def pro(m, ins, extra, x2, _):
        for t in range(2):
            fwd = live_rows(m, t, total_of(ins, t))
            extra[0][pl.ds(t * half_leaf, half_leaf), :] = fwd
            put(x2, 0, t * half_leaf, fwd)

    terms, (leaf_fwd,) = leaf_phase(meta0, leaf_below, terms[0] + terms[1], pro, [(local, width)], stay=False)
    contrib = [-sum(terms[t]) for t in range(2)]

    pieces, offsets = [], []
    for t in range(2):
        bufs, offs = [contrib[t]], [0]
        for m in reversed(z_masks):
            bufs, offs = bufs + [over_sub(b, m) for b in bufs], offs + [o ^ m for o in offs]
        pieces += bufs
        offsets += [(t, o) for o in offs]

    part = (half_fronts * mid_rows, width)

    def assemble(m, *refs):
        ins, outs = refs[:-2], refs[-2:]
        for out in outs:
            out[...] = jnp.zeros_like(out)
        for ref, (t, off) in zip(ins, offsets):
            leaf = m[at["self"]] ^ off
            for j in range(per_stream):
                row = m[at["pivot"] + leaf * 2 * per_stream + t * per_stream + j]

                for h, out in enumerate(outs):
                    at_row = row - h * part[0]

                    @pl.when((at_row >= 0) & (at_row < part[0]))
                    def _():
                        rows = pl.ds(pl.multiple_of(at_row, sub), sub)
                        out[rows, :] += ref[pl.ds(j * sub, sub), :]

    pivot_mine = pl.pallas_call(
        assemble,
        out_shape=[jax.ShapeDtypeStruct(part, F32)] * 2,
        grid_spec=pltpu.PrefetchScalarGridSpec(
            num_scalar_prefetch=1,
            grid=(1,),
            in_specs=[pl.BlockSpec(p.shape, lambda i, m: (0, 0)) for p in pieces],
            out_specs=[pl.BlockSpec(part, lambda i, m: (0, 0))] * 2,
        ),
        compiler_params=pltpu.CompilerParams(vmem_limit_bytes=VMEM_LIMIT),
        name="pivot_rows",
    )(meta, *pieces)
    pivot_other = [over_sub(x, 1) for x in pivot_mine]
    mid_flat = mid_rhs.reshape(fronts * mid_rows, width)

    def front_products(matrix, prologue, ins, extra=(), stay=False):
        made, x2, extras = [], None, ()
        for c in range(CUTS):
            res = matmul(
                meta, matrix, matrix.shape[1] // CUTS, fronts, width,
                lambda g, m, c=c: (g, c), ins if c == 0 else [], prologue=prologue, slots=fronts,
                extra=extra if c == 0 else (), x2=x2, keep_x2=c == 0, stay=stay and c == 0,
            )
            made.append(res[:fronts])
            if c == 0:
                extras, x2 = res[fronts:-1], res[-1]
        results = []
        for t in range(2):
            own = range(t * half_fronts, (t + 1) * half_fronts)
            values = [made[c][p] for p in own for c in range(CUTS)]
            results.append(sum_front(values, f_masks[t]))
        return results, extras

    def pro(m, ins, extra, x2, _):
        for p in range(fronts):
            t, q = divmod(p, half_fronts)
            rows = pl.ds(q * mid_rows, mid_rows)
            value = ins[0][pl.ds(p * mid_rows, mid_rows), :] + (ins[1 + t][rows, :] + ins[3 + t][rows, :])
            put(x2, p, 0, value)

    mid_fwd, _ = front_products(mid_lower, pro, [mid_flat, *pivot_mine, *pivot_other], stay=False)

    def core_products(matrix, prologue_of, ins, finish_of=None, sign=1.0):
        results = []
        for flip in (1, 0):
            results.append(matmul(
                meta, matrix, matrix.shape[1], half_fronts, width,
                lambda g, m, flip=flip: ((m[at["core"]] ^ flip) * half_fronts + g, 0), ins,
                prologue=prologue_of(flip), slots=half_fronts, sign=sign,
                finish=finish_of(flip) if finish_of else None,
                order=leave_first(half_fronts, matrix.shape[1]),
            ))
        return sum_subtree(*results)

    own_rows = mid_lower.shape[1]
    n_parts = half_fronts * CUTS

    def pro_of(flip):
        def pro(m, ins, extra, x2, _):
            for t in range(2):

                @pl.when((m[at["core"]] ^ flip) == t)
                def _():
                    for n in range(n_parts):
                        value = ins[2 * (t * n_parts + n)][...] + ins[2 * (t * n_parts + n) + 1][...]
                        put(x2, n // CUTS, n % CUTS * (own_rows // CUTS), value)

        return pro

    def finish_of(flip):
        def finish(m, ins, outs):
            first = (m[at["core"]] ^ flip) * (half_fronts * mid_rows)
            for u in range(2 * per_stream):
                row = m[at["update"] + u] - first

                @pl.when((row >= 0) & (row < half_fronts * mid_rows))
                def _():
                    size = half_fronts * mid_rows // n_pieces
                    to = ((row // size) ^ m[at["flip"]]) * size + row % size
                    rows = pl.ds(pl.multiple_of(to, sub), sub)
                    src = ins[4 * n_parts + u // per_stream]
                    outs[0][rows, :] += src[pl.ds((u % per_stream) * sub, sub), :]

        return finish

    fwd_terms = [*mid_fwd[0], *mid_fwd[1]]
    mine, other = core_products(mid_below, pro_of, fwd_terms + contrib, finish_of, sign=-1.0)

    def root_pro(m, ins, extra, x2, scr):
        total = scr[0]
        total[...] = ins[0][...]
        for n, start in piece_starts(m, half_fronts * mid_rows):
            src = ins[1 + n]
            for k in range(src.shape[0] // block):
                slot = m[at["root"] + start // block + k]
                rows = pl.ds(pl.multiple_of(slot * block, block), block)
                total[rows, :] += src[pl.ds(k * block, block), :]
        put(x2, 0, 0, total[...])

    out_rows = root_lower.shape[0] // 2
    matrix = root_lower[None]
    made, x2 = [], None
    for c in range(CUTS):
        res = matmul(
            meta, matrix, out_rows // CUTS, 1, width,
            lambda q, m, c=c: (0, q * CUTS + c), [root_rhs, *mine, *other] if c == 0 else [],
            prologue=root_pro, x2=x2, keep_x2=c == 0, blocks=2,
            scratch=[pltpu.VMEM((root_rows, width), F32)] if c == 0 else [],
        )
        made.append(res[:2])
        x2 = res[2] if c == 0 else x2
    root_fwd = []
    for t in range(2):
        root_fwd += sum_front([made[c][t] for c in range(CUTS)], f_masks[t])

    def pro(m, ins, extra, x2, _):
        for n in range(2 * CUTS):
            put(x2, 0, n * (out_rows // CUTS), ins[2 * n][...] + ins[2 * n + 1][...])

    matrix = root_upper[None]
    half_root = root_rows // 2
    up_rows = half_root // Z_STREAMS
    sends, keeps, x2 = [], [], None
    for t in range(Z_STREAMS):
        for flip, into in ((1, sends), (0, keeps)):
            res = matmul(
                meta, matrix, up_rows, 1, width,
                lambda g, m, t=t, flip=flip: (0, (m[at["core"]] ^ flip) * Z_STREAMS + t),
                root_fwd if x2 is None else [], prologue=pro, x2=x2, keep_x2=x2 is None,
                order=leave_first(1, up_rows, 1 << top),
            )
            into.append(res[0])
            x2 = res[1] if x2 is None else x2
    mine, other = sum_subtree(sends, keeps)

    def place(m, ins, out):
        for n, start in piece_starts(m, out.shape[0] // 2):
            h = ins[n].shape[0]
            out[pl.ds(pl.multiple_of(start, h), h), :] = ins[n][...]

    def pro(m, ins, extra, x2, _):
        place(m, ins, extra[0])
        for p in range(fronts):
            for k in range(mid_width):
                slot = m[at["root"] + p * mid_width + k]
                rows = pl.ds(pl.multiple_of(slot * block, block), block)
                put(x2, p, k * block, extra[0][rows, :])

    mid_ext, (root_sol,) = front_products(mid_right, pro, [*mine, *other], [(root_rows, width)])
    ext_terms = [*mid_ext[0], *mid_ext[1]]

    def pro_of(flip):
        def pro(m, ins, extra, x2, _):
            for t in range(2):

                @pl.when((m[at["core"]] ^ flip) == t)
                def _():
                    for n in range(n_parts):
                        k = 2 * (t * n_parts + n)
                        a, b, c, d = (ins[j][...] for j in (k, k + 1, 4 * n_parts + k, 4 * n_parts + k + 1))
                        put(x2, n // CUTS, n % CUTS * (own_rows // CUTS), (a + b) - (c + d))

        return pro

    mine, other = core_products(mid_upper, pro_of, fwd_terms + ext_terms)

    def pro(m, ins, extra, x2, _):
        place(m, ins, extra[0])
        for u in range(2 * per_stream):
            rows = pl.ds(pl.multiple_of(m[at["ext_row"] + u], sub), sub)

            @pl.when(m[at["ext_root"] + u] == 0)
            def _():
                put(x2, 0, u * sub, extra[0][rows, :])

            @pl.when(m[at["ext_root"] + u] != 0)
            def _():
                put(x2, 0, u * sub, ins[-1][rows, :])

    terms, (mid_sol,) = leaf_phase(
        meta, leaf_right, [*mine, *other, root_sol], pro,
        [(fronts * mid_rows, width)],
    )

    def pro(m, ins, extra, x2, _):
        for t in range(2):
            back = ins[0][pl.ds(t * half_leaf, half_leaf), :] - total_of(ins, t, 1)
            put(x2, 0, t * half_leaf, live_rows(m, t, back))

    terms, _ = leaf_phase(meta0, leaf_upper, [leaf_fwd, *terms[0], *terms[1]], pro)
    leaf_sol = jnp.concatenate([sum(terms[0]), sum(terms[1])], axis=0)
    ids = jnp.arange(local, dtype=jnp.int32)[:, None]
    leaf_sol = jnp.where(ids < meta0[at["live"]], leaf_sol, 0.0)
    return leaf_sol, mid_sol.reshape(mid_rhs.shape), root_sol


def on_device(
    n_sub,
    n_front,
    leaf_rhs,
    mid_rhs,
    root_rhs,
    leaf_lower,
    leaf_below,
    leaf_right,
    leaf_upper,
    mid_lower,
    mid_below,
    mid_right,
    mid_upper,
    root_lower,
    root_upper,
    leaf_parent,
    leaf_sizes,
    leaf_map,
    mid_map,
):
    group = lax.axis_index("subtree").astype(jnp.int32)
    column = lax.axis_index("front").astype(jnp.int32)
    local = leaf_rhs.shape[1]
    scenarios = leaf_rhs.shape[2]
    block = local * n_front // leaf_map.shape[1]
    mid_rows = mid_rhs.shape[1]
    mid_width = mid_rows // block
    root_width = root_rhs.shape[0] // block
    leaf_width = local // block
    sub = min(block, local // 2)
    per_stream = (local // 2) // sub
    f_bits = n_front.bit_length() - 1
    masks = [1 << j for j in range(f_bits)]
    orders = [halving_order(masks), halving_order(masks[::-1])]
    table = [(o, t) for t in range(2) for o in orders[t]]
    order = (column ^ jnp.array([o for o, _ in table], jnp.int32)) * 2
    order = order + jnp.array([t for _, t in table], jnp.int32)
    own_size = lax.dynamic_slice_in_dim(leaf_sizes, group, 1)
    top = n_sub.bit_length() - 3
    flip = (1 << top) - 1
    for j in range(top):
        flip = flip ^ (((group >> (j + 1)) & 1) << (top - 1 - j))
    head = jnp.stack([column, group, group & 1, own_size[0] - column * local, jnp.int32(flip)])
    meta0 = jnp.concatenate([head, order])

    columns = lax.dynamic_slice_in_dim(leaf_map, column * leaf_width, leaf_width, 1)
    starts = [u * sub for u in range(2 * per_stream)]
    blocks = jnp.stack([columns[:, r // block] for r in starts], axis=1)
    inner = jnp.array([r % block for r in starts], jnp.int32)[None]
    halves = n_front * mid_width
    is_update = blocks >= halves
    slot = blocks - jnp.where(is_update, halves, 0) - column * mid_width
    target = leaf_parent[:, None] * mid_rows + slot * block + inner
    pivot = jnp.where(is_update, -1, target)
    update = jnp.where(is_update, target, -(1 << 24))
    root = lax.dynamic_slice_in_dim(mid_map, column * mid_width, mid_width, 1) - column * root_width
    row = lambda a: lax.dynamic_slice_in_dim(a, group, 1, 0)[0]
    own_update, own_slot = row(is_update), row(slot)
    own_parent = row(leaf_parent)
    root_slot = root.reshape(-1)[jnp.clip(own_parent * mid_width + own_slot, 0, root.size - 1)]
    ext_row = jnp.where(own_update, root_slot * block + inner[0], row(target))
    parts = [
        ("pivot", pivot.reshape(-1)),
        ("update", row(update)),
        ("root", root.reshape(-1)),
        ("ext_root", own_update.astype(jnp.int32)),
        ("ext_row", ext_row),
    ]
    at = {"self": 1, "core": 2, "live": 3, "flip": 4, "order": 5}
    at |= {"block": block, "sub": sub, "per_stream": per_stream}
    size = meta0.shape[0]
    for key, value in parts:
        at[key] = size
        size += value.shape[0]
    meta = jnp.concatenate([meta0] + [v.astype(jnp.int32) for _, v in parts])

    width = scenarios // CHAINS
    results = []
    gate = []
    for k in range(CHAINS):
        cols = slice(k * width, (k + 1) * width)
        solved = solve(
            gate,
            n_sub, n_front, (meta0, meta, at),
            leaf_rhs[0][:, cols], mid_rhs[:, :, cols], root_rhs[:, cols],
            leaf_lower, leaf_below, leaf_right, leaf_upper,
            mid_lower, mid_below, mid_right, mid_upper, root_lower, root_upper,
        )
        results.append(solved)
    outs = [jnp.concatenate(r, axis=-1) if CHAINS > 1 else r[0] for r in zip(*results)]
    return outs[0][None], outs[1], outs[2]


def solution(mesh):
    return jax.shard_map(
        functools.partial(on_device, mesh.shape["subtree"], mesh.shape["front"]),
        mesh=mesh,
        in_specs=(
            P("subtree", "front", None),
            P(None, "front", None),
            P("front", None),
            P("subtree", None, "front"),
            P("subtree", None, "front"),
            P("subtree", None, "front"),
            P("subtree", None, "front"),
            P(None, "subtree", "front"),
            P(None, "front", "subtree"),
            P(None, "subtree", "front"),
            P(None, "front", "subtree"),
            P("subtree", "front"),
            P("front", "subtree"),
            P(),
            P(),
            P(),
            P(),
        ),
        out_specs=(P("subtree", "front", None), P(None, "front", None), P("front", None)),
        check_vma=False,
    )
```

```python
import functools

import jax
import jax.numpy as jnp
from jax import lax
from jax.experimental import pallas as pl
from jax.experimental.pallas import tpu as pltpu
from jax.sharding import PartitionSpec as P


F32 = jnp.float32
BF16 = jnp.bfloat16
CHAINS = 1
Z_STREAMS = 2
BLOCK_BYTES = 13 << 18
CUTS = 2
VMEM_LIMIT = 40 << 20


def partner(x, axis, mask, n):
    return lax.ppermute(x, axis, [(i, i ^ mask) for i in range(n)])


def halving_order(masks):
    if not masks:
        return [0]
    rest = halving_order(masks[1:])
    return [masks[0] ^ c for c in rest] + rest


def pick_depth(rows, depth):
    best = depth
    for d in range(128, depth, 128):
        if depth % d == 0 and (rows * d * 4 <= BLOCK_BYTES or d == 128):
            best = d
    if rows * depth * 4 <= BLOCK_BYTES:
        best = depth
    return best


def put(x2, slot, start, value):
    n = value.shape[1]
    rows = pl.ds(start, value.shape[0])
    high = value.astype(BF16)
    x2[slot, rows, pl.ds(0, n)] = high
    x2[slot, rows, pl.ds(n, n)] = (value - high.astype(F32)).astype(BF16)


def product(a, x2):
    n = x2.shape[1] // 2
    high = a.astype(BF16)
    low = (a - high.astype(F32)).astype(BF16)
    both = jnp.dot(high, x2, preferred_element_type=F32)
    return (both[:, :n] + both[:, n:]) + jnp.dot(low, x2[:, :n], preferred_element_type=F32)


def matmul(
    meta,
    matrix,
    rows,
    groups,
    width,
    index,
    ins,
    prologue=None,
    slots=1,
    extra=(),
    x2=None,
    keep_x2=False,
    scratch=(),
    finish=None,
    sign=1.0,
    in_specs=None,
    blocks=1,
    cuts=1,
    order=None,
    stay=False,
):
    depth = matrix.shape[2]
    chunk = pick_depth(rows * blocks, depth)
    steps = depth // chunk
    outs = groups * blocks * cuts if order is None else 1
    piece = rows // cuts
    n_in, n_extra = len(ins), len(extra)
    x2_shape = (slots, depth, 2 * width)
    given = x2 is not None

    def whole(a):
        nd = len(a)
        return pl.BlockSpec(a, lambda g, k, m, nd=nd: (0,) * nd)

    def kernel(meta_ref, *refs):
        g, k = pl.program_id(0), pl.program_id(1)
        a_refs, refs = refs[:blocks], refs[blocks:]
        in_refs, refs = refs[:n_in], refs[n_in:]
        if given:
            x2_ref, refs = refs[0], refs[1:]
        out_refs, refs = refs[:outs], refs[outs:]
        extra_refs, refs = refs[:n_extra], refs[n_extra:]
        if not given:
            x2_ref, refs = refs[0], refs[1:]

            @pl.when((g == 0) & (k == 0))
            def _():
                prologue(meta_ref, in_refs, extra_refs, x2_ref, refs)

        slot = 0 if slots == 1 else g
        part = x2_ref[slot, pl.ds(pl.multiple_of(k * chunk, chunk), chunk), :]
        whole_a = [a[0] for a in a_refs]
        acc = product(whole_a[0] if blocks == 1 else jnp.concatenate(whole_a, axis=0), part)
        if sign != 1.0:
            acc = -acc

        def write(ref, to, value, first):
            ref[to, :] = value if first else ref[to, :] + value

        def store(first):
            if order is not None:
                for start, size, to in order(meta_ref, g):
                    to = pl.ds(pl.multiple_of(to, size), size)
                    write(out_refs[0], to, acc[start : start + size], first)
                return
            for own in range(groups):

                def body():
                    for c in range(blocks * cuts):
                        value = acc[c * piece : (c + 1) * piece]
                        write(out_refs[own * blocks * cuts + c], pl.ds(0, piece), value, first)

                if groups == 1:
                    body()
                else:
                    pl.when(g == own)(body)

        if steps == 1:
            store(True)
        else:
            pl.when(k == 0)(lambda: store(True))
            pl.when(k != 0)(lambda: store(False))

        if finish is not None:

            @pl.when((g == groups - 1) & (k == steps - 1))
            def _():
                finish(meta_ref, in_refs, out_refs)

    out_rows = piece if order is None else groups * rows
    out_shape = [jax.ShapeDtypeStruct((out_rows, width), F32)] * outs
    out_shape += [jax.ShapeDtypeStruct(e, F32) for e in extra]
    out_specs = [whole(o.shape) for o in out_shape]
    scratch_shapes = list(scratch)
    if stay:
        matrix = pltpu.with_memory_space_constraint(matrix, pltpu.HBM)
    args = [matrix] * blocks + list(ins)
    specs = [
        pl.BlockSpec((1, rows, chunk), lambda g, k, m, q=q: (*index(q if groups == 1 else g, m), k))
        for q in range(blocks)
    ]
    specs += in_specs if in_specs is not None else [whole(a.shape) for a in ins]
    if given:
        args.append(x2)
        specs.append(whole(x2_shape))
    elif keep_x2:
        out_shape.append(jax.ShapeDtypeStruct(x2_shape, BF16))
        out_specs.append(whole(x2_shape))
    else:
        scratch_shapes = [pltpu.VMEM(x2_shape, BF16)] + scratch_shapes
    return pl.pallas_call(
        kernel,
        out_shape=out_shape,
        grid_spec=pltpu.PrefetchScalarGridSpec(
            num_scalar_prefetch=1,
            grid=(groups, steps),
            in_specs=specs,
            out_specs=out_specs,
            scratch_shapes=scratch_shapes,
        ),
        compiler_params=pltpu.CompilerParams(
            dimension_semantics=("arbitrary", "arbitrary"), vmem_limit_bytes=VMEM_LIMIT
        ),
        cost_estimate=pl.CostEstimate(
            flops=6 * groups * blocks * rows * depth * width,
            bytes_accessed=4 * groups * blocks * rows * depth,
            transcendentals=0,
        ),
    )(meta, *args)


def solve(
    n_sub,
    n_front,
    tables,
    leaf_rhs,
    mid_rhs,
    root_rhs,
    leaf_lower,
    leaf_below,
    leaf_right,
    leaf_upper,
    mid_lower,
    mid_below,
    mid_right,
    mid_upper,
    root_lower,
    root_upper,
):
    meta0, meta, at = tables
    width = leaf_rhs.shape[1]
    local = leaf_rhs.shape[0]
    fronts, mid_rows = mid_rhs.shape[0], mid_rhs.shape[1]
    root_rows = root_rhs.shape[0]
    block, sub, per_stream = at["block"], at["sub"], at["per_stream"]
    half_leaf = local // 2
    half_fronts = fronts // 2
    mid_width = mid_rows // block
    f_bits = n_front.bit_length() - 1
    z_bits = n_sub.bit_length() - 2
    f_masks = [1 << j for j in range(f_bits)]
    f_masks = [f_masks, f_masks[::-1]]
    z_masks = [2 << j for j in range(z_bits)]
    over_front = lambda x, m: partner(x, "front", m, n_front)
    over_sub = lambda x, m: partner(x, "subtree", m, n_sub)

    def scatter_sum(blocks, masks):
        terms = [[b] for b in blocks]
        for m in masks:
            h = len(terms) // 2
            got = [over_front(sum(b), m) for b in terms[:h]]
            terms = [keep + [g] for keep, g in zip(terms[h:], got)]
        return terms[0]

    def sum_front(values, masks):
        terms = []
        for value in values:
            for m in masks[:-1]:
                got = over_front(value, m)
                value = value + got
            terms += [value, over_front(value, masks[-1])]
        return terms

    top = z_bits - 1
    n_pieces = Z_STREAMS << top

    def sum_subtree(sends, keeps):
        got = [over_sub(x, 1) for x in sends]
        mine, other = [], []
        for t in range(Z_STREAMS):
            if len(keeps) == Z_STREAMS:
                parts = [keeps[t], got[t]]
            else:
                h = keeps[0].shape[0] // Z_STREAMS
                parts = [x[0][t * h : (t + 1) * h] for x in (keeps, got)]
            for j in range(top):
                n = parts[0].shape[0] // 2
                leave = sum(x[:n] for x in parts)
                got_low = over_sub(leave, z_masks[j])
                parts = [sum(x[n:] for x in parts), got_low]
            value = sum(parts)
            crossed = over_sub(value, z_masks[top])
            pieces = [value + crossed]
            for j in reversed(range(top)):
                pieces += [over_sub(p, z_masks[j]) for p in pieces]
            mine += pieces
            other += [over_sub(p, 1) for p in pieces]
        return mine, other

    def leave_first(groups, rows, pieces=n_pieces):
        per = pieces // groups
        size = rows // per

        def order(m, g):
            return [(p * size, size, ((g * per + p) ^ m[at["flip"]]) * size) for p in range(per)]

        return order

    piece_bits = [0]
    for j in reversed(range(top)):
        piece_bits += [o | (1 << j) for o in piece_bits]

    def piece_starts(m, half_rows):
        stream = half_rows // Z_STREAMS
        for w in range(2):
            for t in range(Z_STREAMS):
                for n, off in enumerate(piece_bits):
                    z = (m[at["self"]] // 2) ^ off
                    start = (m[at["core"]] ^ w) * half_rows + t * stream
                    for j in range(top):
                        start = start + ((z >> j) & 1) * (stream >> (j + 1))
                    yield (w * Z_STREAMS + t) * len(piece_bits) + n, start

    def leaf_phase(meta_, matrix, ins, prologue, extra=(), stay=False):
        early = max(n_front // 4, 1)
        spots = [[t * n_front + n for n in range(n_front)] for t in range(2)]
        calls = [spots[0][:early] + spots[1][:early], spots[0][early:] + spots[1][early:]]
        made, extras, x2 = {}, (), None
        for call, chosen in enumerate(calls):

            def pick(q, m, chosen=chosen):
                return 0, m[at["order"] + chosen[q]]

            res = matmul(
                meta_, matrix, half_leaf, 1, width, pick,
                ins if call == 0 else [], prologue=prologue, blocks=len(chosen),
                extra=extra if call == 0 else (), keep_x2=call == 0, x2=x2,
                stay=stay and call == 0,
            )
            made.update(zip(chosen, res))
            if call == 0:
                extras, x2 = res[len(chosen) : -1], res[-1]
        terms = [scatter_sum([made[n] for n in spots[t]], f_masks[t]) for t in range(2)]
        return terms, extras

    def live_rows(m, t, value):
        ids = lax.broadcasted_iota(jnp.int32, value.shape, 0) + t * half_leaf
        return jnp.where(ids < m[at["live"]], value, 0.0)

    def pro(m, ins, extra, x2, _):
        for t in range(2):
            put(x2, 0, t * half_leaf, live_rows(m, t, ins[0][pl.ds(t * half_leaf, half_leaf), :]))

    terms, _ = leaf_phase(meta0, leaf_lower, [leaf_rhs], pro, stay=True)

    n_terms = f_bits + 1

    def total_of(refs, t, skip=0):
        return sum(r[...] for r in refs[skip + t * n_terms : skip + (t + 1) * n_terms])

    def pro(m, ins, extra, x2, _):
        for t in range(2):
            fwd = live_rows(m, t, total_of(ins, t))
            extra[0][pl.ds(t * half_leaf, half_leaf), :] = fwd
            put(x2, 0, t * half_leaf, fwd)

    terms, (leaf_fwd,) = leaf_phase(meta0, leaf_below, terms[0] + terms[1], pro, [(local, width)], stay=True)
    contrib = [-sum(terms[t]) for t in range(2)]

    pieces, offsets = [], []
    for t in range(2):
        bufs, offs = [contrib[t]], [0]
        for m in reversed(z_masks):
            bufs, offs = bufs + [over_sub(b, m) for b in bufs], offs + [o ^ m for o in offs]
        pieces += bufs
        offsets += [(t, o) for o in offs]

    part = (half_fronts * mid_rows, width)

    def assemble(m, *refs):
        ins, outs = refs[:-2], refs[-2:]
        for out in outs:
            out[...] = jnp.zeros_like(out)
        for ref, (t, off) in zip(ins, offsets):
            leaf = m[at["self"]] ^ off
            for j in range(per_stream):
                row = m[at["pivot"] + leaf * 2 * per_stream + t * per_stream + j]

                for h, out in enumerate(outs):
                    at_row = row - h * part[0]

                    @pl.when((at_row >= 0) & (at_row < part[0]))
                    def _():
                        rows = pl.ds(pl.multiple_of(at_row, sub), sub)
                        out[rows, :] += ref[pl.ds(j * sub, sub), :]

    pivot_mine = pl.pallas_call(
        assemble,
        out_shape=[jax.ShapeDtypeStruct(part, F32)] * 2,
        grid_spec=pltpu.PrefetchScalarGridSpec(
            num_scalar_prefetch=1,
            grid=(1,),
            in_specs=[pl.BlockSpec(p.shape, lambda i, m: (0, 0)) for p in pieces],
            out_specs=[pl.BlockSpec(part, lambda i, m: (0, 0))] * 2,
        ),
        compiler_params=pltpu.CompilerParams(vmem_limit_bytes=VMEM_LIMIT),
        name="pivot_rows",
    )(meta, *pieces)
    pivot_other = [over_sub(x, 1) for x in pivot_mine]
    mid_flat = mid_rhs.reshape(fronts * mid_rows, width)

    def front_products(matrix, prologue, ins, extra=(), stay=False):
        made, x2, extras = [], None, ()
        for c in range(CUTS):
            res = matmul(
                meta, matrix, matrix.shape[1] // CUTS, fronts, width,
                lambda g, m, c=c: (g, c), ins if c == 0 else [], prologue=prologue, slots=fronts,
                extra=extra if c == 0 else (), x2=x2, keep_x2=c == 0, stay=stay and c == 0,
            )
            made.append(res[:fronts])
            if c == 0:
                extras, x2 = res[fronts:-1], res[-1]
        results = []
        for t in range(2):
            own = range(t * half_fronts, (t + 1) * half_fronts)
            values = [made[c][p] for p in own for c in range(CUTS)]
            results.append(sum_front(values, f_masks[t]))
        return results, extras

    def pro(m, ins, extra, x2, _):
        for p in range(fronts):
            t, q = divmod(p, half_fronts)
            rows = pl.ds(q * mid_rows, mid_rows)
            value = ins[0][pl.ds(p * mid_rows, mid_rows), :] + (ins[1 + t][rows, :] + ins[3 + t][rows, :])
            put(x2, p, 0, value)

    mid_fwd, _ = front_products(mid_lower, pro, [mid_flat, *pivot_mine, *pivot_other], stay=True)

    def core_products(matrix, prologue_of, ins, finish_of=None, sign=1.0):
        results = []
        for flip in (1, 0):
            results.append(matmul(
                meta, matrix, matrix.shape[1], half_fronts, width,
                lambda g, m, flip=flip: ((m[at["core"]] ^ flip) * half_fronts + g, 0), ins,
                prologue=prologue_of(flip), slots=half_fronts, sign=sign,
                finish=finish_of(flip) if finish_of else None,
                order=leave_first(half_fronts, matrix.shape[1]),
            ))
        return sum_subtree(*results)

    own_rows = mid_lower.shape[1]
    n_parts = half_fronts * CUTS

    def pro_of(flip):
        def pro(m, ins, extra, x2, _):
            for t in range(2):

                @pl.when((m[at["core"]] ^ flip) == t)
                def _():
                    for n in range(n_parts):
                        value = ins[2 * (t * n_parts + n)][...] + ins[2 * (t * n_parts + n) + 1][...]
                        put(x2, n // CUTS, n % CUTS * (own_rows // CUTS), value)

        return pro

    def finish_of(flip):
        def finish(m, ins, outs):
            first = (m[at["core"]] ^ flip) * (half_fronts * mid_rows)
            for u in range(2 * per_stream):
                row = m[at["update"] + u] - first

                @pl.when((row >= 0) & (row < half_fronts * mid_rows))
                def _():
                    size = half_fronts * mid_rows // n_pieces
                    to = ((row // size) ^ m[at["flip"]]) * size + row % size
                    rows = pl.ds(pl.multiple_of(to, sub), sub)
                    src = ins[4 * n_parts + u // per_stream]
                    outs[0][rows, :] += src[pl.ds((u % per_stream) * sub, sub), :]

        return finish

    fwd_terms = [*mid_fwd[0], *mid_fwd[1]]
    mine, other = core_products(mid_below, pro_of, fwd_terms + contrib, finish_of, sign=-1.0)

    def root_pro(m, ins, extra, x2, scr):
        total = scr[0]
        total[...] = ins[0][...]
        for n, start in piece_starts(m, half_fronts * mid_rows):
            src = ins[1 + n]
            for k in range(src.shape[0] // block):
                slot = m[at["root"] + start // block + k]
                rows = pl.ds(pl.multiple_of(slot * block, block), block)
                total[rows, :] += src[pl.ds(k * block, block), :]
        put(x2, 0, 0, total[...])

    out_rows = root_lower.shape[0] // 2
    matrix = root_lower[None]
    made, x2 = [], None
    for c in range(CUTS):
        res = matmul(
            meta, matrix, out_rows // CUTS, 1, width,
            lambda q, m, c=c: (0, q * CUTS + c), [root_rhs, *mine, *other] if c == 0 else [],
            prologue=root_pro, x2=x2, keep_x2=c == 0, blocks=2,
            scratch=[pltpu.VMEM((root_rows, width), F32)] if c == 0 else [],
        )
        made.append(res[:2])
        x2 = res[2] if c == 0 else x2
    root_fwd = []
    for t in range(2):
        root_fwd += sum_front([made[c][t] for c in range(CUTS)], f_masks[t])

    def pro(m, ins, extra, x2, _):
        for n in range(2 * CUTS):
            put(x2, 0, n * (out_rows // CUTS), ins[2 * n][...] + ins[2 * n + 1][...])

    matrix = root_upper[None]
    half_root = root_rows // 2
    up_rows = half_root // Z_STREAMS
    sends, keeps, x2 = [], [], None
    for t in range(Z_STREAMS):
        for flip, into in ((1, sends), (0, keeps)):
            res = matmul(
                meta, matrix, up_rows, 1, width,
                lambda g, m, t=t, flip=flip: (0, (m[at["core"]] ^ flip) * Z_STREAMS + t),
                root_fwd if x2 is None else [], prologue=pro, x2=x2, keep_x2=x2 is None,
                order=leave_first(1, up_rows, 1 << top),
            )
            into.append(res[0])
            x2 = res[1] if x2 is None else x2
    mine, other = sum_subtree(sends, keeps)

    def place(m, ins, out):
        for n, start in piece_starts(m, out.shape[0] // 2):
            h = ins[n].shape[0]
            out[pl.ds(pl.multiple_of(start, h), h), :] = ins[n][...]

    def pro(m, ins, extra, x2, _):
        place(m, ins, extra[0])
        for p in range(fronts):
            for k in range(mid_width):
                slot = m[at["root"] + p * mid_width + k]
                rows = pl.ds(pl.multiple_of(slot * block, block), block)
                put(x2, p, k * block, extra[0][rows, :])

    mid_ext, (root_sol,) = front_products(mid_right, pro, [*mine, *other], [(root_rows, width)])
    ext_terms = [*mid_ext[0], *mid_ext[1]]

    def pro_of(flip):
        def pro(m, ins, extra, x2, _):
            for t in range(2):

                @pl.when((m[at["core"]] ^ flip) == t)
                def _():
                    for n in range(n_parts):
                        k = 2 * (t * n_parts + n)
                        a, b, c, d = (ins[j][...] for j in (k, k + 1, 4 * n_parts + k, 4 * n_parts + k + 1))
                        put(x2, n // CUTS, n % CUTS * (own_rows // CUTS), (a + b) - (c + d))

        return pro

    mine, other = core_products(mid_upper, pro_of, fwd_terms + ext_terms)

    def pro(m, ins, extra, x2, _):
        place(m, ins, extra[0])
        for u in range(2 * per_stream):
            rows = pl.ds(pl.multiple_of(m[at["ext_row"] + u], sub), sub)

            @pl.when(m[at["ext_root"] + u] == 0)
            def _():
                put(x2, 0, u * sub, extra[0][rows, :])

            @pl.when(m[at["ext_root"] + u] != 0)
            def _():
                put(x2, 0, u * sub, ins[-1][rows, :])

    terms, (mid_sol,) = leaf_phase(
        meta, leaf_right, [*mine, *other, root_sol], pro,
        [(fronts * mid_rows, width)],
    )

    def pro(m, ins, extra, x2, _):
        for t in range(2):
            back = ins[0][pl.ds(t * half_leaf, half_leaf), :] - total_of(ins, t, 1)
            put(x2, 0, t * half_leaf, live_rows(m, t, back))

    terms, _ = leaf_phase(meta0, leaf_upper, [leaf_fwd, *terms[0], *terms[1]], pro)
    leaf_sol = jnp.concatenate([sum(terms[0]), sum(terms[1])], axis=0)
    ids = jnp.arange(local, dtype=jnp.int32)[:, None]
    leaf_sol = jnp.where(ids < meta0[at["live"]], leaf_sol, 0.0)
    return leaf_sol, mid_sol.reshape(mid_rhs.shape), root_sol


def on_device(
    n_sub,
    n_front,
    leaf_rhs,
    mid_rhs,
    root_rhs,
    leaf_lower,
    leaf_below,
    leaf_right,
    leaf_upper,
    mid_lower,
    mid_below,
    mid_right,
    mid_upper,
    root_lower,
    root_upper,
    leaf_parent,
    leaf_sizes,
    leaf_map,
    mid_map,
):
    group = lax.axis_index("subtree").astype(jnp.int32)
    column = lax.axis_index("front").astype(jnp.int32)
    local = leaf_rhs.shape[1]
    scenarios = leaf_rhs.shape[2]
    block = local * n_front // leaf_map.shape[1]
    mid_rows = mid_rhs.shape[1]
    mid_width = mid_rows // block
    root_width = root_rhs.shape[0] // block
    leaf_width = local // block
    sub = min(block, local // 2)
    per_stream = (local // 2) // sub
    f_bits = n_front.bit_length() - 1
    masks = [1 << j for j in range(f_bits)]
    orders = [halving_order(masks), halving_order(masks[::-1])]
    table = [(o, t) for t in range(2) for o in orders[t]]
    order = (column ^ jnp.array([o for o, _ in table], jnp.int32)) * 2
    order = order + jnp.array([t for _, t in table], jnp.int32)
    own_size = lax.dynamic_slice_in_dim(leaf_sizes, group, 1)
    top = n_sub.bit_length() - 3
    flip = (1 << top) - 1
    for j in range(top):
        flip = flip ^ (((group >> (j + 1)) & 1) << (top - 1 - j))
    head = jnp.stack([column, group, group & 1, own_size[0] - column * local, jnp.int32(flip)])
    meta0 = jnp.concatenate([head, order])

    columns = lax.dynamic_slice_in_dim(leaf_map, column * leaf_width, leaf_width, 1)
    starts = [u * sub for u in range(2 * per_stream)]
    blocks = jnp.stack([columns[:, r // block] for r in starts], axis=1)
    inner = jnp.array([r % block for r in starts], jnp.int32)[None]
    halves = n_front * mid_width
    is_update = blocks >= halves
    slot = blocks - jnp.where(is_update, halves, 0) - column * mid_width
    target = leaf_parent[:, None] * mid_rows + slot * block + inner
    pivot = jnp.where(is_update, -1, target)
    update = jnp.where(is_update, target, -(1 << 24))
    root = lax.dynamic_slice_in_dim(mid_map, column * mid_width, mid_width, 1) - column * root_width
    row = lambda a: lax.dynamic_slice_in_dim(a, group, 1, 0)[0]
    own_update, own_slot = row(is_update), row(slot)
    own_parent = row(leaf_parent)
    root_slot = root.reshape(-1)[jnp.clip(own_parent * mid_width + own_slot, 0, root.size - 1)]
    ext_row = jnp.where(own_update, root_slot * block + inner[0], row(target))
    parts = [
        ("pivot", pivot.reshape(-1)),
        ("update", row(update)),
        ("root", root.reshape(-1)),
        ("ext_root", own_update.astype(jnp.int32)),
        ("ext_row", ext_row),
    ]
    at = {"self": 1, "core": 2, "live": 3, "flip": 4, "order": 5}
    at |= {"block": block, "sub": sub, "per_stream": per_stream}
    size = meta0.shape[0]
    for key, value in parts:
        at[key] = size
        size += value.shape[0]
    meta = jnp.concatenate([meta0] + [v.astype(jnp.int32) for _, v in parts])

    width = scenarios // CHAINS
    results = []
    for k in range(CHAINS):
        cols = slice(k * width, (k + 1) * width)
        solved = solve(
            n_sub, n_front, (meta0, meta, at),
            leaf_rhs[0][:, cols], mid_rhs[:, :, cols], root_rhs[:, cols],
            leaf_lower, leaf_below, leaf_right, leaf_upper,
            mid_lower, mid_below, mid_right, mid_upper, root_lower, root_upper,
        )
        results.append(solved)
    outs = [jnp.concatenate(r, axis=-1) if CHAINS > 1 else r[0] for r in zip(*results)]
    return outs[0][None], outs[1], outs[2]


def solution(mesh):
    return jax.shard_map(
        functools.partial(on_device, mesh.shape["subtree"], mesh.shape["front"]),
        mesh=mesh,
        in_specs=(
            P("subtree", "front", None),
            P(None, "front", None),
            P("front", None),
            P("subtree", None, "front"),
            P("subtree", None, "front"),
            P("subtree", None, "front"),
            P("subtree", None, "front"),
            P(None, "subtree", "front"),
            P(None, "front", "subtree"),
            P(None, "subtree", "front"),
            P(None, "front", "subtree"),
            P("subtree", "front"),
            P("front", "subtree"),
            P(),
            P(),
            P(),
            P(),
        ),
        out_specs=(P("subtree", "front", None), P(None, "front", None), P("front", None)),
        check_vma=False,
    )
```
